32 devices in a mesh: tm: 2 (over x), space: 16 (over z, y, core).
Axes of the slice: x: 2, y: 2, z: 4, core: 2. Of those that a mesh axis runs over, the one named last changes fastest.
Arguments:
- increment: float32 [4, 5, 48, 128, 128], P('tm', None, None, 'space'), may hold values from -6 to 6
- multiplier: float32 [4, 5, 48, 128, 128], P('tm', None, None, 'space'), may hold values from -20 to 20
- sensor_multiplier: float32 [4, 2048], P('tm'), may hold values from -6 to 6
- misfit: float32 [4, 5, 48, 128, 128], P('tm', None, None, 'space'), may hold values from -20 to 20
- innovation: float32 [4, 2048], P('tm'), may hold values from -6 to 6
- model_error: float32 [5, 48], replicated, may hold values from 0.2 to 1
- sensor_error: float32 [4, 2048], P('tm'), may hold values from 0.3 to 1.5
- trajectory: bfloat16 [4, 2, 2, 48, 128, 128], P('tm', None, None, None, 'space'), may hold values from 0 to 1
- land_sea: int32 [128, 128], P('space'), may hold values 0 or 1
- sensor_cells: int32 [4, 2048], P('tm'), may hold values from 0 to 1572863
Outputs:
- increment_next: float32 [4, 5, 48, 128, 128], P('tm', None, None, 'space')
- multiplier_next: float32 [4, 5, 48, 128, 128], P('tm', None, None, 'space')
- sensor_next: float32 [4, 2048], P('tm')
The draws below stay inside these ranges and needn't reach their ends.
Inputs may be any that keep to these rules, and one draw needn't show every extreme that they name: `sensor_cells`: the flat index ((f * 48 + l) * 128 + x) * 128 + y of the observed cell at field f (0 temperature, 1 salinity), level l, column x, row y; an index may repeat.
All inputs are finite; a program needn't handle non-finite values. No bound on the sum of `land_sea` on one device may be relied on, other than what follows from the above.
Results may differ from the reference program's by a relative error of at most 0.0017.
Values may be sent and summed in bfloat16 or wider, within the bound.
No kernel may reach another device: no remote copies, remote signals or barrier semaphores. Data moves between devices by JAX's collectives and lax.ppermute only.
A program may use at most 64 MiB of HBM per device.

```python
import math
import jax
import jax.numpy as jnp
from jax import lax

NY = 128
LEV = 48
STEPS = 2
NOBS = 2048
SUBWINDOWS = 4
NX = 128


def ramped_field(key, salt_code):
    local_key = jax.random.fold_in(key, salt_code)
    shape = (SUBWINDOWS, 5, LEV, NX, NY)
    timing = jnp.arange(SUBWINDOWS, dtype=jnp.float32) / max(SUBWINDOWS - 1, 1)
    longitude = jnp.arange(NX, dtype=jnp.float32) / max(NX - 1, 1)
    base = jax.random.truncated_normal(local_key, -6.0, 6.0, shape, jnp.float32)
    exponent = 0.5 * timing[:, None, None, None, None] + 0.5 * longitude[None, None, None, :, None]
    return base * 10.0 ** exponent / 3.0


def draw_misfit(key, part):
    return ramped_field(key, 11)


def draw_multiplier(key, part):
    return ramped_field(key, 23)


def set_ends(values, rng, smallest, largest):
    dims = values.shape
    index_at = [jax.random.randint(jax.random.fold_in(rng, axis), (), 0, dims[axis]) for axis in range(len(dims))]
    values = values.at[tuple(index_at)].set(smallest)
    longest = dims.index(max(dims))
    index_at[longest] = (index_at[longest] + 1) % dims[longest]
    return values.at[tuple(index_at)].set(largest)


def block_levels(key, shape, pieces, low, top_value):
    level, own = 1.0, jax.random.fold_in(key, 6)
    for dim, shards_of in pieces:
        heights = jnp.exp(jax.random.uniform(jax.random.fold_in(own, dim), (shards_of,), jnp.float32, low / len(pieces), top_value / len(pieces)))
        level = level * jnp.repeat(heights, shape[dim] // shards_of).reshape([-1 if axis == dim else 1 for axis in range(len(shape))])
    return level


def normal_values(rng, shape, deviation, bound, shards=(), held_as=jnp.bfloat16):
    drawn = deviation * jax.random.normal(rng, shape, jnp.float32)
    if shards:
        drawn = drawn * block_levels(rng, shape, shards, -0.22, 0.18)
    return jnp.clip(drawn, -bound, bound).astype(held_as)


def setup_inputs(seed: int = 0) -> dict:
    key_list = jax.random.split(jax.random.key(seed), 11)
    increment = normal_values(key_list[0], (SUBWINDOWS, 5, LEV, NX, NY), 1.0, 6.0, ((0, 2), (3, 16)), jnp.float32)
    multiplier = draw_multiplier(jax.random.fold_in(key_list[10], 71), 0)
    sensor_multiplier = normal_values(key_list[2], (SUBWINDOWS, NOBS), 1.0, 6.0, ((0, 2),), jnp.float32)
    misfit = draw_misfit(jax.random.fold_in(key_list[10], 71), 0)
    innovation = normal_values(key_list[4], (SUBWINDOWS, NOBS), 1.0, 6.0, ((0, 2),), jnp.float32)
    model_error = jnp.clip(jnp.exp(jax.random.uniform(key_list[5], (5, LEV), jnp.float32, math.log(0.2), math.log(1.0))), 0.2, 1.0)
    sensor_error = jnp.clip(jnp.exp(math.log(1.5) - 1.60943787 * jax.random.uniform(key_list[6], (SUBWINDOWS, NOBS), jnp.float32) ** block_levels(key_list[6], (SUBWINDOWS, NOBS), ((0, 2),), -0.2, 0.2)), 0.3, 1.5)
    trajectory = jnp.clip(1.0 * jax.random.uniform(key_list[7], (SUBWINDOWS, STEPS, 2, LEV, NX, NY), jnp.float32) ** block_levels(key_list[7], (SUBWINDOWS, STEPS, 2, LEV, NX, NY), ((0, 2), (4, 16)), -0.2, 0.2), 0.0, 1.0).astype(jnp.bfloat16)
    land_sea = set_ends((jax.random.randint(key_list[8], (NX, NY), 0, 8) < 7).astype(jnp.int32), jax.random.fold_in(key_list[8], 1), 0, 1)
    sensor_cells = set_ends(jax.random.randint(key_list[9], (SUBWINDOWS, NOBS), 0, 2 * LEV * NX * NY), jax.random.fold_in(key_list[9], 1), 0, (2 * LEV * NX * NY) - 1).astype(jnp.int32)
    return {"increment": increment, "multiplier": multiplier, "sensor_multiplier": sensor_multiplier, "misfit": misfit, "innovation": innovation, "model_error": model_error, "sensor_error": sensor_error, "trajectory": trajectory, "land_sea": land_sea, "sensor_cells": sensor_cells}


thermal_lin = 0.2
thermal_quad = 0.02
haline_lin = 0.8
cabbeling = 0.01
gravity = 1.0
time_stride = 0.3
mixing = 0.15
coriolis = 0.5
relaxation = 0.5
epsilon = 1e-06

def column_pad(values):
    return jnp.pad(values, ((0, 0), (0, 0), (1, 1)))

def tendency(padded, history, landmask):
    temper = 30.0 * history[0] - 10.0
    saline = 8.0 * history[1] - 5.0
    dens_temper = -thermal_lin - thermal_quad * temper + cabbeling * saline
    dens_saline = haline_lin + cabbeling * temper
    density = dens_temper * padded[0] + dens_saline * padded[1]
    pressure = padded[4] + gravity * density
    latitude = padded.shape[3]
    rotation = coriolis * (jnp.arange(latitude, dtype=jnp.float32) - 0.5 * (latitude - 1)) / (0.5 * latitude)

    def middle(f):
        return f[:, 1:-1]

    def zonal_slope(f):
        return 0.5 * (f[:, 2:] - f[:, :-2])

    def meridional_slope(f):
        g = column_pad(middle(f))
        return 0.5 * (g[..., 2:] - g[..., :-2])

    def laplacian(f):
        g = column_pad(middle(f))
        return f[:, 2:] + f[:, :-2] + g[..., 2:] + g[..., :-2] - 4.0 * middle(f)
    heat_next = middle(padded[0]) + mixing * laplacian(padded[0])
    salt_next = middle(padded[1]) + mixing * laplacian(padded[1])
    east_next = middle(padded[2]) + time_stride * (rotation * middle(padded[3]) - zonal_slope(pressure))
    north_next = middle(padded[3]) + time_stride * (-rotation * middle(padded[2]) - meridional_slope(pressure))
    surface_next = middle(padded[4]) - time_stride * (zonal_slope(padded[2]) + meridional_slope(padded[3])) + mixing * laplacian(padded[4])
    return jnp.stack([heat_next, salt_next, east_next, north_next, surface_next]) * landmask

def wrap_columns(values):
    return jnp.concatenate([values[..., -1:, :], values, values[..., :1, :]], axis=-2)

def propagate(initial, history, landmask):
    fields = initial
    for j in range(STEPS):
        fields = tendency(wrap_columns(fields), wrap_columns(history[j]), landmask)
    return fields

def adjoint(cotangent, history, landmask):
    _, pull = jax.vjp(lambda v: propagate(v, history, landmask), jnp.zeros_like(cotangent))
    return pull(cotangent)[0]

def reference(increment, multiplier, sensor_multiplier, misfit, innovation, model_error, sensor_error, trajectory, land_sea, sensor_cells):
    landmask = land_sea.astype(jnp.float32)
    history = trajectory.astype(jnp.float32)
    forward = lax.map(lambda p: propagate(p[0], p[1], landmask), (increment, history))
    previous = jnp.concatenate([jnp.zeros_like(forward[:1]), forward[:-1]], axis=0)
    damping = model_error[None, :, :, None, None]
    model_residual = misfit - damping * multiplier - (increment - previous)
    multiplier_next = multiplier + relaxation * model_residual
    flattened = increment[:, :2].reshape(increment.shape[0], -1)
    observed = jnp.take_along_axis(flattened, sensor_cells, axis=1)
    sensor_residual = innovation - sensor_error * sensor_multiplier - observed
    sensor_next = sensor_multiplier + relaxation * sensor_residual
    following = jnp.concatenate([multiplier_next[1:], jnp.zeros_like(multiplier_next[:1])], axis=0)
    returned = lax.map(lambda p: adjoint(p[0], p[1], landmask), (following, history))
    subwindow_rows = jnp.arange(flattened.shape[0], dtype=jnp.int32)[:, None]
    spread = jnp.zeros_like(flattened).at[subwindow_rows, sensor_cells].add(sensor_next)
    spread = spread.reshape(increment[:, :2].shape)
    sensor_part = jnp.concatenate([spread, jnp.zeros_like(increment[:, 2:])], axis=1)
    gradient = multiplier_next - returned + sensor_part
    misfit_square = jnp.sum(model_residual * model_residual) + jnp.sum(sensor_residual * sensor_residual)
    gradient_square = jnp.sum(gradient * gradient)
    stride = misfit_square / (gradient_square + epsilon)
    return (increment - stride * gradient, multiplier_next, sensor_next)
```

```python
import jax
import jax.numpy as jnp
from jax import lax
from jax.experimental import pallas as pl
from jax.experimental.pallas import tpu as pltpu
from jax.sharding import PartitionSpec as P

thermal_lin = 0.2
thermal_quad = 0.02
haline_lin = 0.8
cabbeling = 0.01
gravity = 1.0
time_stride = 0.3
mixing = 0.15
coriolis = 0.5
relaxation = 0.5
epsilon = 1e-06

kt0 = -thermal_lin + 10.0 * thermal_quad - 5.0 * cabbeling
kt1 = -30.0 * thermal_quad
kt2 = 8.0 * cabbeling
ks0 = haline_lin - 10.0 * cabbeling
ks1 = 30.0 * cabbeling
half = 0.5 * time_stride

LB = 16
TE, SA, U, V, PR = range(5)
F32 = jnp.float32
BF16 = jnp.bfloat16

NEAR = {TE: 0, SA: 1, U: 2, V: 3, PR: 4}
FAR = {TE: 5, SA: 6, U: 7, PR: 8}
BACK = 9
QN, QF, H0, H1 = 9, 10, 11, 12
AHEAD = 13


def rows_of(ref, lead, col, width):
    return ref[lead + (pl.ds(col, LB, stride=width), slice(None))]


def dens(h0, h1):
    return kt0 + kt1 * h0 + kt2 * h1, ks0 + ks1 * h0


class Rows:
    def __init__(self, latitude):
        lane = lax.broadcasted_iota(jnp.int32, (LB, latitude), 1)
        self.n = latitude
        self.first = lane == 0
        self.last = lane == latitude - 1
        row = lane.astype(F32)
        self.rot = (time_stride * coriolis / (0.5 * latitude)) * (row - 0.5 * (latitude - 1))

    def up(self, f):
        return jnp.where(self.last, 0.0, pltpu.roll(f, self.n - 1, 1))

    def down(self, f):
        return jnp.where(self.first, 0.0, pltpu.roll(f, 1, 1))

    def diff(self, f):
        return self.up(f) - self.down(f)

    def both(self, f):
        return self.up(f) + self.down(f)


def pack_kernel(inc_ref, traj_ref, land_ref, up_ref, dn_ref, h_s):
    subs, width = inc_ref.shape[0], land_ref.shape[0]
    for k in range(subs):
        for j in range(2):
            for s in range(2):
                h_s[2 * j + s] = traj_ref[k, j, s].astype(F32)
        for out, near, far in ((up_ref, width - 1, width - 2), (dn_ref, 0, 1)):
            base = AHEAD * k
            for col, planes, q in ((near, NEAR, QN), (far, FAR, QF)):
                vals = {f: rows_of(inc_ref, (k, f), col, width) for f in planes}
                for f, p in planes.items():
                    out[base + p] = vals[f].astype(BF16)
                kt, ks = dens(rows_of(h_s, (0,), col, width), rows_of(h_s, (1,), col, width))
                out[base + q] = (vals[PR] + gravity * (kt * vals[TE] + ks * vals[SA])).astype(BF16)
            out[base + H0] = rows_of(h_s, (2,), near, width).astype(BF16)
            out[base + H1] = rows_of(h_s, (3,), near, width).astype(BF16)
    for out, near in ((up_ref, width - 1), (dn_ref, 0)):
        mask = land_ref[near : near + 1, :].astype(F32)
        out[AHEAD * subs] = jnp.broadcast_to(mask, (LB, mask.shape[1])).astype(BF16)


def partial_kernel(inc_ref, mult_ref, misfit_ref, damp_ref, edge_ref, inner_ref):
    fields, width = inc_ref.shape[1], edge_ref.shape[1] + inner_ref.shape[1]
    for f in range(fields):
        damp = damp_ref[f]
        for c in range(width):
            mult = rows_of(mult_ref, (0, f), c, width)
            base = rows_of(misfit_ref, (0, f), c, width) - damp * mult - rows_of(inc_ref, (0, f), c, width)
            value = (mult + relaxation * base).astype(BF16)
            if 2 <= c < width - 2:
                inner_ref[f, c - 2] = value
            else:
                edge_ref[f, c if c < 2 else c - width + 4] = value


def sensor_kernel(inc_ref, row_ref, lat_ref, mult_ref, innov_ref, err_ref, obs_ref, spread_ref, sum_ref, acc_s):
    subs, rows, latitude = inc_ref.shape[0], 2 * inc_ref.shape[2], inc_ref.shape[3]
    nobs = row_ref.shape[1]
    blk = 512 if nobs % 512 == 0 else nobs
    total = jnp.zeros((1, blk), F32)
    for k in range(subs):
        flat = jnp.concatenate([inc_ref[k, 0], inc_ref[k, 1]], axis=0)
        flat_t = flat.T
        hi = flat_t.astype(BF16)
        lo = (flat_t - hi.astype(F32)).astype(BF16)
        left = jnp.concatenate([hi, lo], axis=0)
        for b in range(nobs // blk):
            span = pl.ds(b * blk, blk)
            row = row_ref[k : k + 1, span]
            lat = lat_ref[k : k + 1, span]
            hot = jnp.where(lax.broadcasted_iota(jnp.int32, (rows, blk), 0) == row, 1.0, 0.0).astype(BF16)
            here = lax.broadcasted_iota(jnp.int32, (latitude, blk), 0) == lat
            both = jnp.dot(left, hot, preferred_element_type=F32)
            seen = jnp.sum(jnp.where(here, both[:latitude] + both[latitude:], 0.0), axis=0, keepdims=True)
            mult = mult_ref[k : k + 1, span]
            resid = innov_ref[k : k + 1, span] - err_ref[k : k + 1, span] * mult - seen
            nxt = mult + relaxation * resid
            total = total + jnp.where(row >= 0, resid * resid, 0.0)
            nhi = nxt.astype(BF16).astype(F32)
            nlo = nxt - nhi
            right = jnp.concatenate([jnp.where(here, nhi, 0.0), jnp.where(here, nlo, 0.0)], axis=0).astype(BF16)
            add = lax.dot_general(hot, right, (((1,), (1,)), ((), ())), preferred_element_type=F32)
            if b == 0:
                acc_s[...] = add
            else:
                acc_s[...] += add
            obs_ref[k : k + 1, span] = seen
        spread_ref[k] = acc_s[:, :latitude] + acc_s[:, latitude:]
    sum_ref[...] = total


def forward_kernel(
    keep_ref, inc_ref, traj_ref, land_ref, left_ref, right_ref, mult_ref, misfit_ref, damp_ref, edge_ref,
    fwd_ref, send_ref, mult_out, up_ref, dn_ref, sum_ref, x_s, y_s, q_s, h_s,
):
    subs, fields, width, latitude = inc_ref.shape[0], inc_ref.shape[1], land_ref.shape[0], land_ref.shape[1]
    lanes = Rows(latitude)
    keep = keep_ref[0, 0]

    def mask_at(c):
        if c < 0:
            return left_ref[AHEAD * subs].astype(F32)
        if c >= width:
            return right_ref[AHEAD * subs].astype(F32)
        return jnp.broadcast_to(land_ref[c : c + 1, :].astype(F32), (LB, latitude))

    @pl.when(pl.program_id(0) == 0)
    def _():
        sum_ref[...] = jnp.zeros_like(sum_ref)

    total = jnp.zeros((LB, latitude), F32)
    for k in reversed(range(subs)):
        base = AHEAD * k
        for j in range(2):
            for s in range(2):
                h_s[2 * j + s] = traj_ref[k, j, s].astype(F32)
        for c in range(width):
            for f in range(fields):
                x_s[f, c + 2] = rows_of(inc_ref, (k, f), c, width)
            kt, ks = dens(rows_of(h_s, (0,), c, width), rows_of(h_s, (1,), c, width))
            q_s[c + 2] = x_s[PR, c + 2] + gravity * (kt * x_s[TE, c + 2] + ks * x_s[SA, c + 2])
        for ref, near, far in ((left_ref, 1, 0), (right_ref, width + 2, width + 3)):
            for f, p in NEAR.items():
                x_s[f, near] = ref[base + p].astype(F32)
            for f, p in FAR.items():
                x_s[f, far] = ref[base + p].astype(F32)
            q_s[near] = ref[base + QN].astype(F32)
            q_s[far] = ref[base + QF].astype(F32)

        def substep(src, q, i, mask, with_v):
            te, sa, u, v, pr = (src[f, i] for f in range(5))
            lap = lambda f, x: src[f, i + 1] + src[f, i - 1] + lanes.both(x)
            centre = 1.0 - 4.0 * mixing
            heat = mask * (centre * te + mixing * lap(TE, te))
            salt = mask * (centre * sa + mixing * lap(SA, sa))
            east = mask * (u + lanes.rot * v - half * (q[i + 1] - q[i - 1]))
            north = mask * (v - lanes.rot * u - half * lanes.diff(q[i])) if with_v else None
            surf = mask * (
                centre * pr + mixing * lap(PR, pr) - half * (src[U, i + 1] - src[U, i - 1] + lanes.diff(v))
            )
            return heat, salt, east, north, surf

        for c in range(-1, width + 1):
            inside = 0 <= c < width
            new = substep(x_s, q_s, c + 2, mask_at(c), inside)
            for f in range(5):
                if new[f] is not None:
                    y_s[f, c + 2] = new[f]
            if inside:
                h0, h1 = rows_of(h_s, (2,), c, width), rows_of(h_s, (3,), c, width)
            else:
                ref = left_ref if c < 0 else right_ref
                h0, h1 = ref[base + H0].astype(F32), ref[base + H1].astype(F32)
            kt, ks = dens(h0, h1)
            y_s[5, c + 2] = new[PR] + gravity * (kt * new[TE] + ks * new[SA])
        for c in range(width):
            mask = mask_at(c)
            new = substep(y_s, y_s.at[5], c + 2, mask, True)
            for f in range(fields):
                if k == subs - 1:
                    fwd_ref[f, c] = new[f]
                    send_ref[f, c] = new[f].astype(BF16)
                    if c < 2 or c >= width - 2:
                        got = edge_ref[f, c if c < 2 else c - width + 4].astype(F32)
                        after = mask * (keep * (got + relaxation * new[f]))
                else:
                    mult = rows_of(mult_ref, (0, f), c, width)
                    resid = (
                        rows_of(misfit_ref, (0, f), c, width)
                        - damp_ref[f] * mult
                        - (rows_of(inc_ref, (k + 1, f), c, width) - new[f])
                    )
                    total = total + resid * resid
                    after = mult + relaxation * resid
                    mult_out[f, c] = after
                    after = mask * after
                where = BACK * k
                if c == width - 1:
                    up_ref[where + NEAR[f]] = after.astype(BF16)
                if c == width - 2 and f != V:
                    up_ref[where + FAR[f]] = after.astype(BF16)
                if c == 0:
                    dn_ref[where + NEAR[f]] = after.astype(BF16)
                if c == 1 and f != V:
                    dn_ref[where + FAR[f]] = after.astype(BF16)
    sum_ref[...] += total


def adjoint_kernel(
    keep_ref, inc_ref, traj_ref, land_ref, left_ref, right_ref, backl_ref, backr_ref, mult_ref, misfit_ref, damp_ref,
    fwd_ref, mnext_ref, edge_ref, inner_ref, prev_ref, spread_ref, sumf_ref, sums_ref,
    mult_out, grad_ref, tot_ref, x_s, y_s, h_s, acc_s,
):
    subs, fields, width, latitude = traj_ref.shape[0], mult_ref.shape[1], land_ref.shape[0], land_ref.shape[1]
    lanes = Rows(latitude)
    keep = keep_ref[0, 0]

    def mask_at(c):
        if c < 0:
            return left_ref[AHEAD * subs].astype(F32)
        if c >= width:
            return right_ref[AHEAD * subs].astype(F32)
        return jnp.broadcast_to(land_ref[c : c + 1, :].astype(F32), (LB, latitude))

    @pl.when(pl.program_id(0) == 0)
    def _():
        acc_s[...] = jnp.zeros_like(acc_s)

    misfit_total = jnp.zeros((LB, latitude), F32)
    grad_total = jnp.zeros((LB, latitude), F32)
    for k in range(subs):
        for j in range(2):
            for s in range(2):
                h_s[2 * j + s] = traj_ref[k, j, s].astype(F32)
        for c in range(width):
            mask = mask_at(c)
            for f in range(fields):
                if k == subs - 1:
                    got = inner_ref[f, c - 2] if 2 <= c < width - 2 else edge_ref[f, c if c < 2 else c - width + 4]
                    x_s[f, c + 2] = mask * (keep * (got.astype(F32) + relaxation * fwd_ref[f, c]))
                else:
                    x_s[f, c + 2] = mask * mnext_ref[f, c]
        for ref, near, far in ((backl_ref, 1, 0), (backr_ref, width + 2, width + 3)):
            for f, p in NEAR.items():
                x_s[f, near] = ref[BACK * k + p].astype(F32)
            for f, p in FAR.items():
                x_s[f, far] = ref[BACK * k + p].astype(F32)

        def back(src, i, h0, h1, with_v):
            te, sa, u, v, pr = (src[f, i] for f in range(5))
            kt, ks = dens(h0, h1)
            centre = 1.0 - 4.0 * mixing
            mix = lambda f, x: centre * x + mixing * (src[f, i + 1] + src[f, i - 1] + lanes.both(x))
            q = half * (src[U, i + 1] - src[U, i - 1] + lanes.diff(v))
            gq = gravity * q
            heat = mix(TE, te) + kt * gq
            salt = mix(SA, sa) + ks * gq
            east = u - lanes.rot * v + half * (src[PR, i + 1] - src[PR, i - 1])
            north = v + lanes.rot * u + half * lanes.diff(pr) if with_v else None
            surf = mix(PR, pr) + q
            return heat, salt, east, north, surf

        for c in range(-1, width + 1):
            inside = 0 <= c < width
            if inside:
                h0, h1 = rows_of(h_s, (2,), c, width), rows_of(h_s, (3,), c, width)
            else:
                ref = left_ref if c < 0 else right_ref
                h0, h1 = ref[AHEAD * k + H0].astype(F32), ref[AHEAD * k + H1].astype(F32)
            mask = mask_at(c)
            new = back(x_s, c + 2, h0, h1, inside)
            for f in range(5):
                if new[f] is not None:
                    y_s[f, c + 2] = mask * new[f]
        for c in range(width):
            new = back(y_s, c + 2, rows_of(h_s, (0,), c, width), rows_of(h_s, (1,), c, width), True)
            for f in range(fields):
                if k == 0:
                    mult = rows_of(mult_ref, (0, f), c, width)
                    resid = (
                        rows_of(misfit_ref, (0, f), c, width)
                        - damp_ref[f] * mult
                        - (rows_of(inc_ref, (0, f), c, width) - prev_ref[f, c].astype(F32))
                    )
                    misfit_total = misfit_total + resid * resid
                    value = mult + relaxation * resid
                else:
                    value = mnext_ref[f, c]
                mult_out[k, f, pl.ds(c, LB, stride=width), :] = value
                grad = value - new[f]
                if f < 2:
                    grad = grad + rows_of(spread_ref, (k, f), c, width)
                grad_total = grad_total + grad * grad
                grad_ref[k, f, pl.ds(c, LB, stride=width), :] = grad
    acc_s[0] += misfit_total
    acc_s[1] += grad_total

    @pl.when(pl.program_id(0) == pl.num_programs(0) - 1)
    def _():
        misfit_sum = jnp.sum(acc_s[0] + sumf_ref[...]) + jnp.sum(sums_ref[...])
        grad_sum = jnp.sum(acc_s[1])
        lane = lax.broadcasted_iota(jnp.int32, tot_ref.shape, 1)
        tot_ref[...] = jnp.where(lane == 0, misfit_sum, jnp.where(lane == 1, grad_sum, 0.0))


def step_kernel(recv_ref, inc_ref, grad_ref, out_ref):
    misfit_square = jnp.sum(recv_ref[:, 0:1])
    gradient_square = jnp.sum(recv_ref[:, 1:2])
    top = jnp.full((1, 128), misfit_square, F32)
    stride = top / (jnp.full((1, 128), gradient_square, F32) + epsilon)
    stride = stride[0, 0]
    out_ref[...] = inc_ref[...] - stride * grad_ref[...]


def shifted(shard, axis, by):
    peers = lax.axis_size(axis)
    pairs = [(i, i + by) for i in range(peers) if 0 <= i + by < peers]
    return lax.ppermute(shard, axis, pairs)


def around(shard, axis, by):
    peers = lax.axis_size(axis)
    return lax.ppermute(shard, axis, [(i, (i + by) % peers) for i in range(peers)])


def whole(shape):
    return pl.BlockSpec(shape, lambda i: (0,) * len(shape))


def on_device(
    increment, multiplier, sensor_multiplier, misfit, innovation,
    model_error, sensor_error, trajectory, land_sea, sensor_cells,
):
    subs, fields, levels, width, latitude = increment.shape
    nobs = sensor_cells.shape[1]
    teams, tiles = lax.axis_size("tm"), lax.axis_size("space")
    assert fields == 5 and trajectory.shape[1] == 2 and subs == 2 and levels % LB == 0 and width >= 4
    rows = levels * width
    steps = levels // LB
    block = LB * width
    inc = increment.reshape(subs, fields, rows, latitude)
    mult = multiplier.reshape(subs, fields, rows, latitude)
    mis = misfit.reshape(subs, fields, rows, latitude)
    traj = trajectory.reshape(subs, 2, 2, rows, latitude)
    damp = jnp.broadcast_to(model_error[:, :, None], (fields, levels, latitude))
    keep = jnp.where(lax.axis_index("tm") < teams - 1, 1.0, 0.0).astype(F32).reshape(1, 1)

    def call(kernel, name, ins, outs, scratch):
        return pl.pallas_call(
            kernel,
            name=name,
            grid=(steps,),
            in_specs=ins,
            out_specs=[o[0] for o in outs],
            out_shape=[o[1] for o in outs],
            scratch_shapes=scratch,
        )

    shape = jax.ShapeDtypeStruct
    smem = pl.BlockSpec((1, 1), lambda i: (0, 0), memory_space=pltpu.SMEM)
    state = lambda n, first=0: pl.BlockSpec((n, fields, block, latitude), lambda i: (first, 0, i, 0))
    saved = pl.BlockSpec((subs, 2, 2, block, latitude), lambda i: (0, 0, 0, i, 0))
    planes = lambda n: pl.BlockSpec((n, LB, latitude), lambda i: (0, i, 0))
    columns = lambda n: pl.BlockSpec((fields, n, LB, latitude), lambda i: (0, 0, i, 0))
    damping = pl.BlockSpec((fields, LB, latitude), lambda i: (0, i, 0))
    land = whole((width, latitude))
    scr = lambda *s: pltpu.VMEM(s, F32)

    ahead = subs * AHEAD + 1
    up, dn = call(
        pack_kernel, "pack",
        [state(subs), saved, land],
        [(planes(ahead), shape((ahead, levels, latitude), BF16))] * 2,
        [scr(4, block, latitude)],
    )(inc, traj, land_sea)
    left = around(up, "space", 1)
    right = around(dn, "space", -1)

    edge, inner = call(
        partial_kernel, "partial",
        [state(1), state(1), state(1), damping],
        [
            (columns(4), shape((fields, 4, levels, latitude), BF16)),
            (columns(width - 4), shape((fields, width - 4, levels, latitude), BF16)),
        ],
        [],
    )(inc, mult, mis, damp)
    edge_in = shifted(edge, "tm", -1)
    inner_in = shifted(inner, "tm", -1)

    plane = width * tiles * latitude
    offset = lax.axis_index("space") * width
    field_level = sensor_cells // plane
    remainder = sensor_cells % plane
    column = remainder // latitude - offset
    owned = (column >= 0) & (column < width)
    row_index = jnp.where(owned, field_level * width + column, -1)
    lat_index = remainder % latitude
    full = lambda *s: pl.BlockSpec(s, lambda i: (0,) * len(s))
    observed, spread, sensor_sum = pl.pallas_call(
        sensor_kernel,
        name="sensor",
        grid=(1,),
        in_specs=[full(subs, 2, rows, latitude)] + [full(subs, nobs)] * 5,
        out_specs=[full(subs, nobs), full(subs, 2 * rows, latitude), full(1, 512 if nobs % 512 == 0 else nobs)],
        out_shape=[
            shape((subs, nobs), F32),
            shape((subs, 2 * rows, latitude), F32),
            shape((1, 512 if nobs % 512 == 0 else nobs), F32),
        ],
        scratch_shapes=[scr(2 * rows, 2 * latitude)],
    )(inc, row_index, lat_index, sensor_multiplier, innovation, sensor_error)
    spread = spread.reshape(subs, 2, rows, latitude)

    fwd, send, mnext, back_up, back_dn, forward_sum = call(
        forward_kernel, "forward",
        [smem, state(subs), saved, land, planes(ahead), planes(ahead), state(1, 1), state(1, 1), damping, columns(4)],
        [
            (columns(width), shape((fields, width, levels, latitude), F32)),
            (columns(width), shape((fields, width, levels, latitude), BF16)),
            (columns(width), shape((fields, width, levels, latitude), F32)),
            (planes(subs * BACK), shape((subs * BACK, levels, latitude), BF16)),
            (planes(subs * BACK), shape((subs * BACK, levels, latitude), BF16)),
            (whole((LB, latitude)), shape((LB, latitude), F32)),
        ],
        [scr(5, width + 4, LB, latitude), scr(6, width + 4, LB, latitude), scr(width + 4, LB, latitude), scr(4, block, latitude)],
    )(keep, inc, traj, land_sea, left, right, mult, mis, damp, edge_in)
    back_left = around(back_up, "space", 1)
    back_right = around(back_dn, "space", -1)
    prev = shifted(send, "tm", 1)

    share = nobs // tiles
    pieces = observed.reshape(subs, tiles, share).transpose(1, 0, 2).reshape(tiles, -1, 128)
    pieces = jnp.sum(lax.all_to_all(pieces, "space", 0, 0), axis=0)

    mult_next, gradient, totals = call(
        adjoint_kernel, "adjoint",
        [
            smem, state(1), saved, land, planes(ahead), planes(ahead), planes(subs * BACK), planes(subs * BACK),
            state(1), state(1), damping, columns(width), columns(width), columns(4), columns(width - 4), columns(width),
            pl.BlockSpec((subs, 2, block, latitude), lambda i: (0, 0, i, 0)),
            whole((LB, latitude)), whole(sensor_sum.shape),
        ],
        [
            (state(subs), shape((subs, fields, rows, latitude), F32)),
            (state(subs), shape((subs, fields, rows, latitude), F32)),
            (whole((1, 128)), shape((1, 128), F32)),
        ],
        [scr(5, width + 4, LB, latitude), scr(5, width + 4, LB, latitude), scr(4, block, latitude), scr(2, LB, latitude)],
    )(
        keep, inc, traj, land_sea, left, right, back_left, back_right, mult, mis, damp,
        fwd, mnext, edge_in, inner_in, prev, spread, forward_sum, sensor_sum,
    )

    final = jnp.concatenate([totals, pieces], axis=0)
    final = jnp.broadcast_to(final[None], (teams * tiles,) + final.shape)
    final = lax.all_to_all(final, ("tm", "space"), 0, 0)

    increment_next = call(
        step_kernel, "step",
        [whole((teams * tiles, 128)), state(subs), state(subs)],
        [(state(subs), shape((subs, fields, rows, latitude), F32))],
        [],
    )(final[:, 0], inc, gradient)[0]

    mine = lax.dynamic_slice_in_dim(final, lax.axis_index("tm") * tiles, tiles, axis=0)[:, 1:]
    whole_obs = mine.reshape(tiles, subs, share).transpose(1, 0, 2).reshape(subs, nobs)
    sensor_next = sensor_multiplier + relaxation * (innovation - sensor_error * sensor_multiplier - whole_obs)
    return (increment_next.reshape(increment.shape), mult_next.reshape(multiplier.shape), sensor_next)


def solution(mesh):
    state = P("tm", None, None, "space", None)
    placed = (
        state,
        state,
        P("tm", None),
        state,
        P("tm", None),
        P(),
        P("tm", None),
        P("tm", None, None, None, "space", None),
        P("space", None),
        P("tm", None),
    )
    return jax.shard_map(
        on_device,
        mesh=mesh,
        in_specs=placed,
        out_specs=(state, state, P("tm", None)),
        check_vma=False,
    )
```

```python
import jax
import jax.numpy as jnp
from jax import lax
from jax.experimental import pallas as pl
from jax.experimental.pallas import tpu as pltpu
from jax.sharding import PartitionSpec as P

thermal_lin = 0.2
thermal_quad = 0.02
haline_lin = 0.8
cabbeling = 0.01
gravity = 1.0
time_stride = 0.3
mixing = 0.15
coriolis = 0.5
relaxation = 0.5
epsilon = 1e-06

kt0 = -thermal_lin + 10.0 * thermal_quad - 5.0 * cabbeling
kt1 = -30.0 * thermal_quad
kt2 = 8.0 * cabbeling
ks0 = haline_lin - 10.0 * cabbeling
ks1 = 30.0 * cabbeling
half = 0.5 * time_stride

LB = 16
VMEM_LIMIT = 16 * 1024 * 1024
TE, SA, U, V, PR = range(5)
F32 = jnp.float32
BF16 = jnp.bfloat16

NEAR = {TE: 0, SA: 1, U: 2, V: 3, PR: 4}
FAR = {TE: 5, SA: 6, U: 7, PR: 8}
BACK = 9
QN, QF, H0, H1 = 9, 10, 11, 12
AHEAD = 13


def rows_of(ref, lead, block, col, width):
    return ref[lead + (pl.ds(block * (LB * width) + col, LB, stride=width), slice(None))]


def dens(h0, h1):
    return kt0 + kt1 * h0 + kt2 * h1, ks0 + ks1 * h0


class Rows:
    def __init__(self, latitude):
        lane = lax.broadcasted_iota(jnp.int32, (LB, latitude), 1)
        self.n = latitude
        self.first = lane == 0
        self.last = lane == latitude - 1
        row = lane.astype(F32)
        self.rot = (time_stride * coriolis / (0.5 * latitude)) * (row - 0.5 * (latitude - 1))

    def up(self, f):
        return jnp.where(self.last, 0.0, pltpu.roll(f, self.n - 1, 1))

    def down(self, f):
        return jnp.where(self.first, 0.0, pltpu.roll(f, 1, 1))

    def diff(self, f):
        return self.up(f) - self.down(f)

    def both(self, f):
        return self.up(f) + self.down(f)


def blocks_of(levels, body):
    lax.fori_loop(0, levels // LB, lambda b, carry: (body(b), carry)[1], 0)


def at(block):
    return pl.ds(pl.multiple_of(block * LB, LB), LB)


def native(block, width):
    size = LB * width
    return pl.ds(pl.multiple_of(block * size, size), size)


def load_kernel(
    error_ref, inc_hbm, traj_hbm, mult_hbm, misfit_hbm, land_ref,
    inc_ref, traj_ref, mult_ref, misfit_ref, up_ref, dn_ref, edge_ref, inner_ref, damp_ref, h_s, sems,
):
    subs, fields, width, levels, latitude = inc_ref.shape[0], inc_ref.shape[1], land_ref.shape[0], up_ref.shape[1], land_ref.shape[1]
    level = lax.broadcasted_iota(jnp.int32, (LB, latitude), 0)

    def copies(b):
        rows = native(b, width)
        first = [
            pltpu.make_async_copy(inc_hbm.at[:, :, rows], inc_ref.at[:, :, rows], sems.at[0, b]),
            pltpu.make_async_copy(traj_hbm.at[:, :, :, rows], traj_ref.at[:, :, :, rows], sems.at[1, b]),
        ]
        second = [
            pltpu.make_async_copy(mult_hbm.at[0, :, rows], mult_ref.at[:, rows], sems.at[2, b]),
            pltpu.make_async_copy(misfit_hbm.at[0, :, rows], misfit_ref.at[:, rows], sems.at[3, b]),
        ]
        return first, second

    for part in range(2):
        for b in range(levels // LB):
            for c in copies(b)[part]:
                c.start()

    def ahead(b):
        for c in copies(b)[0]:
            c.wait()
        for k in range(subs):
            for j in range(2):
                for s in range(2):
                    h_s[2 * j + s] = traj_ref[k, j, s, native(b, width), :].astype(F32)
            for out, near, far in ((up_ref, width - 1, width - 2), (dn_ref, 0, 1)):
                base = AHEAD * k
                for col, planes, q in ((near, NEAR, QN), (far, FAR, QF)):
                    vals = {f: rows_of(inc_ref, (k, f), b, col, width) for f in planes}
                    for f, p in planes.items():
                        out[base + p, at(b), :] = vals[f].astype(BF16)
                    kt, ks = dens(rows_of(h_s, (0,), 0, col, width), rows_of(h_s, (1,), 0, col, width))
                    out[base + q, at(b), :] = (vals[PR] + gravity * (kt * vals[TE] + ks * vals[SA])).astype(BF16)
                out[base + H0, at(b), :] = rows_of(h_s, (2,), 0, near, width).astype(BF16)
                out[base + H1, at(b), :] = rows_of(h_s, (3,), 0, near, width).astype(BF16)
        for out, near in ((up_ref, width - 1), (dn_ref, 0)):
            mask = land_ref[near : near + 1, :].astype(F32)
            out[AHEAD * subs, at(b), :] = jnp.broadcast_to(mask, (LB, mask.shape[1])).astype(BF16)

    def partial(b):
        for f in range(fields):
            damp = jnp.zeros((LB, latitude), F32)
            for i in range(LB):
                damp = jnp.where(level == i, error_ref[f, b * LB + i], damp)
            damp_ref[f, at(b), :] = damp
        for c in copies(b)[1]:
            c.wait()
        for f in range(fields):
            damp = damp_ref[f, at(b), :]
            for c in range(width):
                mult = rows_of(mult_ref, (f,), b, c, width)
                resid = rows_of(misfit_ref, (f,), b, c, width) - damp * mult - rows_of(inc_ref, (0, f), b, c, width)
                value = (mult + relaxation * resid).astype(BF16)
                if 2 <= c < width - 2:
                    inner_ref[f, c - 2, at(b), :] = value
                else:
                    edge_ref[f, c if c < 2 else c - width + 4, at(b), :] = value

    blocks_of(levels, ahead)
    blocks_of(levels, partial)


def prepare_kernel(traj_ref, mult_hbm, misfit_hbm, dens_ref, mult_ref, misfit_ref, h_s, sems):
    subs, width, levels = dens_ref.shape[0], dens_ref.shape[3], dens_ref.shape[4]
    copies = [
        pltpu.make_async_copy(mult_hbm.at[1], mult_ref, sems.at[0]),
        pltpu.make_async_copy(misfit_hbm.at[1], misfit_ref, sems.at[1]),
    ]
    for c in copies:
        c.start()

    def body(b):
        for k in range(subs):
            for j in range(2):
                for s in range(2):
                    h_s[s] = traj_ref[k, j, s, native(b, width), :].astype(F32)
                for c in range(width):
                    kt, ks = dens(rows_of(h_s, (0,), 0, c, width), rows_of(h_s, (1,), 0, c, width))
                    dens_ref[k, j, 0, c, at(b), :] = kt
                    dens_ref[k, j, 1, c, at(b), :] = ks

    blocks_of(levels, body)
    for c in copies:
        c.wait()


def sensor_kernel(inc_ref, cell_ref, mult_ref, innov_ref, err_ref, obs_ref, spread_ref, sum_ref, hot_s, acc_s, *, width, columns):
    subs, rows, latitude = inc_ref.shape[0], 2 * inc_ref.shape[2], inc_ref.shape[3]
    nobs = cell_ref.shape[1]
    peers, share = obs_ref.shape[0], obs_ref.shape[1]
    tiles = subs * nobs // (128 * share)
    blk = 512
    small = 32
    lat_bits = latitude.bit_length() - 1
    col_bits = columns.bit_length() - 1
    offset = lax.axis_index("space") * width
    total = jnp.zeros((1, blk), F32)
    for k in range(subs):
        flat_t = jnp.concatenate([inc_ref[k, 0], inc_ref[k, 1]], axis=0).T
        hi = flat_t.astype(BF16)
        lo = (flat_t - hi.astype(F32)).astype(BF16)
        left = jnp.concatenate([hi, lo], axis=0)
        for b in range(nobs // blk):
            span = slice(b * blk, (b + 1) * blk)
            cell = cell_ref[k : k + 1, span]
            lat = cell & (latitude - 1)
            column = (lax.shift_right_logical(cell, lat_bits) & (columns - 1)) - offset
            owned = (column >= 0) & (column < width)
            row = jnp.where(owned, lax.shift_right_logical(cell, lat_bits + col_bits) * width + column, -1)
            fine = jnp.where(lax.broadcasted_iota(jnp.int32, (small, blk), 0) == (row & (small - 1)), 1.0, 0.0).astype(BF16)
            group = lax.shift_right_arithmetic(row, small.bit_length() - 1)
            for i in range(rows // small):
                coarse = jnp.broadcast_to(jnp.where(group == i, 1.0, 0.0), (small, blk)).astype(BF16)
                hot_s[i * small : (i + 1) * small, :] = coarse * fine
            hot = hot_s[...]
            here = lax.broadcasted_iota(jnp.int32, (latitude, blk), 0) == lat
            both = jnp.dot(left, hot, preferred_element_type=F32)
            seen = jnp.sum(jnp.where(here, both[:latitude] + both[latitude:], 0.0), axis=0, keepdims=True)
            mult = mult_ref[k : k + 1, span]
            resid = innov_ref[k : k + 1, span] - err_ref[k : k + 1, span] * mult - seen
            nxt = mult + relaxation * resid
            total = total + jnp.where(owned, resid * resid, 0.0)
            nhi = nxt.astype(BF16).astype(F32)
            nlo = nxt - nhi
            right = jnp.concatenate([jnp.where(here, nhi, 0.0), jnp.where(here, nlo, 0.0)], axis=0).astype(BF16)
            add = lax.dot_general(hot, right, (((1,), (1,)), ((), ())), preferred_element_type=F32)
            if b == 0:
                acc_s[...] = add
            else:
                acc_s[...] += add
            for i in range(blk // 128):
                g = (k * nobs + b * blk) // 128 + i
                for t in range(peers // tiles):
                    obs_ref[t * tiles + g // share, g % share : g % share + 1, :] = seen[:, i * 128 : (i + 1) * 128]
        spread_ref[k] = acc_s[:, :latitude] + acc_s[:, latitude:]
    sum_ref[...] = total


def keeper(axis):
    return jnp.where(lax.axis_index(axis) < lax.axis_size(axis) - 1, 1.0, 0.0).astype(F32)


def forward_kernel(
    inc_ref, dens_ref, land_ref, left_ref, right_ref, mult_ref, misfit_ref, damp_ref, edge_ref, sensor_ref,
    fwd_ref, send_ref, mult_out, up_ref, dn_ref, sum_ref, x_s, y_s, q_s,
):
    subs, fields, width, latitude = inc_ref.shape[0], inc_ref.shape[1], land_ref.shape[0], land_ref.shape[1]
    levels = fwd_ref.shape[2]
    lanes = Rows(latitude)
    keep = keeper("tm")
    centre = 1.0 - 4.0 * mixing
    sum_ref[...] = jnp.zeros_like(sum_ref)
    sum_ref[0:1, :] = jnp.full((1, latitude), jnp.sum(sensor_ref[...]) / latitude, F32)

    def body(b):
        def mask_at(c):
            if c < 0:
                return left_ref[AHEAD * subs, at(b), :].astype(F32)
            if c >= width:
                return right_ref[AHEAD * subs, at(b), :].astype(F32)
            return jnp.broadcast_to(land_ref[c : c + 1, :].astype(F32), (LB, latitude))

        total = jnp.zeros((LB, latitude), F32)
        for k in reversed(range(subs)):
            base = AHEAD * k
            for c in range(width):
                for f in range(fields):
                    x_s[f, c + 2] = rows_of(inc_ref, (k, f), b, c, width)
                kt, ks = dens_ref[k, 0, 0, c, at(b), :], dens_ref[k, 0, 1, c, at(b), :]
                q_s[c + 2] = x_s[PR, c + 2] + gravity * (kt * x_s[TE, c + 2] + ks * x_s[SA, c + 2])
            for ref, near, far in ((left_ref, 1, 0), (right_ref, width + 2, width + 3)):
                for f, p in NEAR.items():
                    x_s[f, near] = ref[base + p, at(b), :].astype(F32)
                for f, p in FAR.items():
                    x_s[f, far] = ref[base + p, at(b), :].astype(F32)
                q_s[near] = ref[base + QN, at(b), :].astype(F32)
                q_s[far] = ref[base + QF, at(b), :].astype(F32)

            def substep(src, q, i, mask, with_v):
                te, sa, u, v, pr = (src[f, i] for f in range(5))
                stay, swap = centre * mask, mixing * mask
                thrust = half * mask
                heat = stay * te + swap * (src[TE, i + 1] + src[TE, i - 1] + lanes.both(te))
                salt = stay * sa + swap * (src[SA, i + 1] + src[SA, i - 1] + lanes.both(sa))
                east = mask * (u + lanes.rot * v) - thrust * (q[i + 1] - q[i - 1])
                north = mask * (v - lanes.rot * u) - thrust * lanes.diff(q[i]) if with_v else None
                if mixing == half:
                    around_p = lanes.up(pr - v) + lanes.down(pr + v)
                    around_p = around_p + (src[PR, i + 1] + src[PR, i - 1]) - (src[U, i + 1] - src[U, i - 1])
                    surf = stay * pr + swap * around_p
                else:
                    surf = stay * pr + swap * (src[PR, i + 1] + src[PR, i - 1] + lanes.both(pr))
                    surf = surf - thrust * (src[U, i + 1] - src[U, i - 1] + lanes.diff(v))
                return heat, salt, east, north, surf

            for c in range(-1, width + 1):
                inside = 0 <= c < width
                new = substep(x_s, q_s, c + 2, mask_at(c), inside)
                for f in range(5):
                    if new[f] is not None:
                        y_s[f, c + 2] = new[f]
                if inside:
                    kt, ks = dens_ref[k, 1, 0, c, at(b), :], dens_ref[k, 1, 1, c, at(b), :]
                else:
                    ref = left_ref if c < 0 else right_ref
                    kt, ks = dens(ref[base + H0, at(b), :].astype(F32), ref[base + H1, at(b), :].astype(F32))
                y_s[5, c + 2] = new[PR] + gravity * (kt * new[TE] + ks * new[SA])
            for c in range(width):
                mask = mask_at(c)
                new = substep(y_s, y_s.at[5], c + 2, mask, True)
                for f in range(fields):
                    if k == subs - 1:
                        fwd_ref[f, c, at(b), :] = new[f]
                        send_ref[f, c, at(b), :] = new[f].astype(BF16)
                        if c < 2 or c >= width - 2:
                            got = edge_ref[f, c if c < 2 else c - width + 4, at(b), :].astype(F32)
                            after = mask * (keep * (got + relaxation * new[f]))
                    else:
                        mult = rows_of(mult_ref, (f,), b, c, width)
                        resid = (
                            rows_of(misfit_ref, (f,), b, c, width)
                            - damp_ref[f, at(b), :] * mult
                            - (rows_of(inc_ref, (k + 1, f), b, c, width) - new[f])
                        )
                        total = total + resid * resid
                        after = mult + relaxation * resid
                        mult_out[f, c, at(b), :] = after
                        after = mask * after
                    where = BACK * k
                    if c == width - 1:
                        up_ref[where + NEAR[f], at(b), :] = after.astype(BF16)
                    if c == width - 2 and f != V:
                        up_ref[where + FAR[f], at(b), :] = after.astype(BF16)
                    if c == 0:
                        dn_ref[where + NEAR[f], at(b), :] = after.astype(BF16)
                    if c == 1 and f != V:
                        dn_ref[where + FAR[f], at(b), :] = after.astype(BF16)
        sum_ref[...] += total

    blocks_of(levels, body)


def adjoint_kernel(
    inc_ref, dens_ref, land_ref, left_ref, right_ref, backl_ref, backr_ref, mult_ref, misfit_ref, damp_ref,
    fwd_ref, mnext_ref, edge_ref, inner_ref, prev_ref, spread_ref, sum_ref, seen_ref,
    mult_out, grad_ref, fin_ref, x_s, y_s, acc_s,
):
    subs, fields, width, latitude = dens_ref.shape[0], mult_ref.shape[0], land_ref.shape[0], land_ref.shape[1]
    levels = fwd_ref.shape[2]
    lanes = Rows(latitude)
    keep = keeper("tm")
    centre = 1.0 - 4.0 * mixing
    b = pl.program_id(0)

    @pl.when(b == 0)
    def _():
        acc_s[...] = jnp.zeros_like(acc_s)

    def body():
        def mask_at(c):
            if c < 0:
                return left_ref[AHEAD * subs, at(b), :].astype(F32)
            if c >= width:
                return right_ref[AHEAD * subs, at(b), :].astype(F32)
            return jnp.broadcast_to(land_ref[c : c + 1, :].astype(F32), (LB, latitude))

        misfit_total = jnp.zeros((LB, latitude), F32)
        grad_total = jnp.zeros((LB, latitude), F32)
        for k in range(subs):
            for c in range(width):
                mask = mask_at(c)
                for f in range(fields):
                    if k == subs - 1:
                        if 2 <= c < width - 2:
                            got = inner_ref[f, c - 2, at(b), :]
                        else:
                            got = edge_ref[f, c if c < 2 else c - width + 4, at(b), :]
                        value = keep * (got.astype(F32) + relaxation * fwd_ref[f, c, at(b), :])
                    else:
                        value = mnext_ref[f, c, at(b), :]
                    x_s[f, c + 2] = mask * value
            for ref, near, far in ((backl_ref, 1, 0), (backr_ref, width + 2, width + 3)):
                for f, p in NEAR.items():
                    x_s[f, near] = ref[BACK * k + p, at(b), :].astype(F32)
                for f, p in FAR.items():
                    x_s[f, far] = ref[BACK * k + p, at(b), :].astype(F32)

            def back(src, i, kt, ks, with_v):
                te, sa, u, v, pr = (src[f, i] for f in range(5))
                mix = lambda f, x: centre * x + mixing * (src[f, i + 1] + src[f, i - 1] + lanes.both(x))
                q = half * (src[U, i + 1] - src[U, i - 1] + lanes.diff(v))
                gq = gravity * q if gravity != 1.0 else q
                heat = mix(TE, te) + kt * gq
                salt = mix(SA, sa) + ks * gq
                east = u - lanes.rot * v + half * (src[PR, i + 1] - src[PR, i - 1])
                north = v + lanes.rot * u + half * lanes.diff(pr) if with_v else None
                surf = mix(PR, pr) + q
                return heat, salt, east, north, surf

            for c in range(-1, width + 1):
                inside = 0 <= c < width
                if inside:
                    kt, ks = dens_ref[k, 1, 0, c, at(b), :], dens_ref[k, 1, 1, c, at(b), :]
                else:
                    ref = left_ref if c < 0 else right_ref
                    kt, ks = dens(
                        ref[AHEAD * k + H0, at(b), :].astype(F32), ref[AHEAD * k + H1, at(b), :].astype(F32)
                    )
                mask = mask_at(c)
                new = back(x_s, c + 2, kt, ks, inside)
                for f in range(5):
                    if new[f] is not None:
                        y_s[f, c + 2] = mask * new[f]
            for c in range(width):
                new = back(y_s, c + 2, dens_ref[k, 0, 0, c, at(b), :], dens_ref[k, 0, 1, c, at(b), :], True)
                for f in range(fields):
                    if k == 0:
                        mult = rows_of(mult_ref, (f,), b, c, width)
                        resid = (
                            rows_of(misfit_ref, (f,), b, c, width)
                            - damp_ref[f, at(b), :] * mult
                            - (rows_of(inc_ref, (0, f), b, c, width) - prev_ref[f, c, at(b), :].astype(F32))
                        )
                        misfit_total = misfit_total + resid * resid
                        value = mult + relaxation * resid
                    else:
                        value = mnext_ref[f, c, at(b), :]
                    spot = pl.ds(b * (LB * width) + c, LB, stride=width)
                    mult_out[k, f, pl.ds(c, LB, stride=width), :] = value
                    grad = value - new[f]
                    if f < 2:
                        grad = grad + rows_of(spread_ref, (k, f), b, c, width)
                    grad_total = grad_total + grad * grad
                    grad_ref[k, f, spot, :] = grad
        acc_s[0] += misfit_total
        acc_s[1] += grad_total

    body()

    @pl.when(b == pl.num_programs(0) - 1)
    def _():
        misfit_sum = jnp.sum(acc_s[0] + sum_ref[...])
        grad_sum = jnp.sum(acc_s[1])
        lane = lax.broadcasted_iota(jnp.int32, (1, 128), 1)
        scalars = jnp.where(lane == 0, misfit_sum, jnp.where(lane == 1, grad_sum, 0.0))
        tiles = lax.axis_size("space")
        mine = seen_ref[pl.ds(lax.axis_index("tm") * tiles, tiles)]
        pieces = jnp.sum(mine, axis=0)
        peers = fin_ref.shape[0]
        for i in range(peers):
            fin_ref[i, 0:1, :] = scalars
            fin_ref[i, 1:, :] = pieces


def step_kernel(recv_ref, inc_ref, grad_ref, mult_ref, innov_ref, err_ref, out_ref, next_ref, *, steps):
    parts = recv_ref[:, 0, :]
    sums = jnp.sum(parts, axis=0, keepdims=True)
    lane = lax.broadcasted_iota(jnp.int32, sums.shape, 1)
    misfit_square = jnp.sum(jnp.where(lane == 0, sums, 0.0), axis=1, keepdims=True)
    gradient_square = jnp.sum(jnp.where(lane == 1, sums, 0.0), axis=1, keepdims=True)
    stride = misfit_square / (gradient_square + epsilon)
    size = out_ref.shape[2]
    b = pl.program_id(0)
    spot = pl.ds(pl.multiple_of(b * size, size), size)
    for k in range(inc_ref.shape[0]):
        for f in range(inc_ref.shape[1]):
            out_ref[k, f] = inc_ref[k, f, spot, :] - stride * grad_ref[k, f, spot, :]

    @pl.when(b == 0)
    def _():
        subs, nobs = mult_ref.shape
        share = recv_ref.shape[1] - 1
        first = lax.axis_index("tm") * lax.axis_size("space")
        for k in range(subs):
            for i in range(nobs // 128):
                g = k * (nobs // 128) + i
                span = slice(i * 128, (i + 1) * 128)
                seen = recv_ref[first + g // share, 1 + g % share : 2 + g % share, :]
                mult = mult_ref[k : k + 1, span]
                resid = innov_ref[k : k + 1, span] - err_ref[k : k + 1, span] * mult - seen
                next_ref[k : k + 1, span] = mult + relaxation * resid


def shifted(shard, axis, by):
    peers = lax.axis_size(axis)
    pairs = [(i, i + by) for i in range(peers) if 0 <= i + by < peers]
    return lax.ppermute(shard, axis, pairs)


def around(shard, axis, by):
    peers = lax.axis_size(axis)
    return lax.ppermute(shard, axis, [(i, (i + by) % peers) for i in range(peers)])


def on_device(
    increment, multiplier, sensor_multiplier, misfit, innovation,
    model_error, sensor_error, trajectory, land_sea, sensor_cells,
):
    subs, fields, levels, width, latitude = increment.shape
    nobs = sensor_cells.shape[1]
    teams, tiles = lax.axis_size("tm"), lax.axis_size("space")
    peers = teams * tiles
    share = subs * nobs // (128 * tiles)
    assert fields == 5 and trajectory.shape[1] == 2 and subs == 2 and levels % LB == 0 and width >= 4
    assert latitude == 128 and (width * tiles) & (width * tiles - 1) == 0 and nobs % 512 == 0
    assert share * 128 * tiles == subs * nobs and (2 * levels * width) % 32 == 0
    rows = levels * width
    fast = lambda x: pltpu.with_memory_space_constraint(x, pltpu.VMEM)
    slow = lambda x: pltpu.with_memory_space_constraint(x, pltpu.HBM)
    native_shape = (subs, fields, rows, latitude)
    inc = slow(increment.reshape(native_shape))
    traj = slow(trajectory.reshape(subs, 2, 2, rows, latitude))
    mult = slow(multiplier.reshape(native_shape))
    mis = slow(misfit.reshape(native_shape))
    land = fast(land_sea)
    cells, sen_m, sen_i, sen_e = (fast(x) for x in (sensor_cells, sensor_multiplier, innovation, sensor_error))
    vmem = pl.BlockSpec(memory_space=pltpu.VMEM)
    smem = pl.BlockSpec(memory_space=pltpu.SMEM)
    hbm = pl.BlockSpec(memory_space=pltpu.HBM)
    scr = lambda *s: pltpu.VMEM(s, F32)
    limit = pltpu.CompilerParams(vmem_limit_bytes=VMEM_LIMIT)

    def call(kernel, name, outs, scratch, *args, specs=None):
        return pl.pallas_call(
            kernel,
            name=name,
            in_specs=specs or [vmem] * len(args),
            out_specs=[vmem] * len(outs),
            out_shape=[pltpu.VMEM(s, d) for s, d in outs],
            scratch_shapes=scratch,
            compiler_params=limit,
        )(*args)

    ahead = (subs * AHEAD + 1, levels, latitude)
    one = native_shape[1:]
    inc, traj, mult0, mis0, up, dn, edge, inner, damp = call(
        load_kernel, "load",
        [
            (native_shape, F32), (traj.shape, BF16), (one, F32), (one, F32), (ahead, BF16), (ahead, BF16),
            ((fields, 4, levels, latitude), BF16),
            ((fields, width - 4, levels, latitude), BF16),
            ((fields, levels, latitude), F32),
        ],
        [scr(4, LB * width, latitude), pltpu.SemaphoreType.DMA((4, levels // LB))],
        model_error, inc, traj, mult, mis, land,
        specs=[smem] + [hbm] * 4 + [vmem],
    )
    left = fast(around(up, "space", 1))
    right = fast(around(dn, "space", -1))
    edge_in = fast(shifted(edge, "tm", -1))
    inner_in = fast(shifted(inner, "tm", -1))

    density, mult1, mis1 = call(
        prepare_kernel, "prepare",
        [((subs, 2, 2, width, levels, latitude), F32), (one, F32), (one, F32)],
        [scr(2, LB * width, latitude), pltpu.SemaphoreType.DMA((2,))],
        traj, mult, mis,
        specs=[vmem, hbm, hbm],
    )

    seen, spread, sensor_sum = call(
        lambda *refs: sensor_kernel(*refs, width=width, columns=width * tiles), "sensor",
        [((peers, share, 128), F32), ((subs, 2 * rows, latitude), F32), ((1, 512), F32)],
        [pltpu.VMEM((2 * rows, 512), BF16), scr(2 * rows, 2 * latitude)],
        inc, cells, sen_m, sen_i, sen_e,
    )
    spread = spread.reshape(subs, 2, rows, latitude)
    seen_in = fast(lax.all_to_all(seen, ("tm", "space"), 0, 0))

    column = (fields, width, levels, latitude)
    behind = (subs * BACK, levels, latitude)
    fwd, send, mnext, back_up, back_dn, sums = call(
        forward_kernel, "forward",
        [(column, F32), (column, BF16), (column, F32), (behind, BF16), (behind, BF16), ((LB, latitude), F32)],
        [scr(5, width + 4, LB, latitude), scr(6, width + 4, LB, latitude), scr(width + 4, LB, latitude)],
        inc, density, land, left, right, mult1, mis1, damp, edge_in, sensor_sum,
    )
    back_left = fast(around(back_up, "space", 1))
    back_right = fast(around(back_dn, "space", -1))
    prev = fast(shifted(send, "tm", 1))

    block = pl.BlockSpec((subs, fields, LB * width, latitude), lambda i: (0, 0, i, 0))
    mult_next, gradient, final = pl.pallas_call(
        adjoint_kernel,
        name="adjoint",
        grid=(levels // LB,),
        in_specs=[vmem] * 18,
        out_specs=[block, vmem, vmem],
        out_shape=[
            jax.ShapeDtypeStruct(native_shape, F32),
            pltpu.VMEM(native_shape, F32),
            pltpu.VMEM((peers, 1 + share, 128), F32),
        ],
        scratch_shapes=[scr(5, width + 4, LB, latitude), scr(5, width + 4, LB, latitude), scr(2, LB, latitude)],
        compiler_params=limit,
    )(
        inc, density, land, left, right, back_left, back_right, mult0, mis0, damp,
        fwd, mnext, edge_in, inner_in, prev, spread, sums, seen_in,
    )
    final = fast(lax.all_to_all(final, ("tm", "space"), 0, 0))

    steps = 4 if rows % 32 == 0 else 1
    size = rows // steps
    increment_next, sensor_next = pl.pallas_call(
        lambda *refs: step_kernel(*refs, steps=steps),
        name="step",
        grid=(steps,),
        in_specs=[vmem] * 6,
        out_specs=[
            pl.BlockSpec((subs, fields, size, latitude), lambda i: (0, 0, i, 0)),
            pl.BlockSpec((subs, nobs), lambda i: (0, 0)),
        ],
        out_shape=[
            jax.ShapeDtypeStruct(native_shape, F32),
            jax.ShapeDtypeStruct((subs, nobs), F32),
        ],
        compiler_params=limit,
    )(final, inc, gradient, sen_m, sen_i, sen_e)
    return (increment_next.reshape(increment.shape), mult_next.reshape(multiplier.shape), sensor_next)


def solution(mesh):
    state = P("tm", None, None, "space", None)
    placed = (
        state,
        state,
        P("tm", None),
        state,
        P("tm", None),
        P(),
        P("tm", None),
        P("tm", None, None, None, "space", None),
        P("space", None),
        P("tm", None),
    )
    return jax.shard_map(
        on_device,
        mesh=mesh,
        in_specs=placed,
        out_specs=(state, state, P("tm", None)),
        check_vma=False,
    )
```

```python
import jax
import jax.numpy as jnp
from jax import lax
from jax.experimental import pallas as pl
from jax.experimental.pallas import tpu as pltpu
from jax.sharding import PartitionSpec as P


thermal_lin = 0.2
thermal_quad = 0.02
haline_lin = 0.8
cabbeling = 0.01
gravity = 1.0
time_stride = 0.3
mixing = 0.15
coriolis = 0.5
relaxation = 0.5
epsilon = 1e-06

kt0 = -thermal_lin + 10.0 * thermal_quad - 5.0 * cabbeling
kt1 = -30.0 * thermal_quad
kt2 = 8.0 * cabbeling
ks0 = haline_lin - 10.0 * cabbeling
ks1 = 30.0 * cabbeling
half = 0.5 * time_stride

LB = 16
VMEM_LIMIT = 16 * 1024 * 1024
TE, SA, U, V, PR = range(5)
F32 = jnp.float32
BF16 = jnp.bfloat16

NEAR = {TE: 0, SA: 1, U: 2, V: 3, PR: 4}
FAR = {TE: 5, SA: 6, U: 7, PR: 8}
BACK = 9
QN, QF, H0, H1 = 9, 10, 11, 12
AHEAD = 13


def rows_of(ref, lead, block, col, width):
    return ref[lead + (pl.ds(block * (LB * width) + col, LB, stride=width), slice(None))]


def dens(h0, h1):
    return kt0 + kt1 * h0 + kt2 * h1, ks0 + ks1 * h0


class Rows:
    def __init__(self, latitude):
        lane = lax.broadcasted_iota(jnp.int32, (LB, latitude), 1)
        self.n = latitude
        self.first = lane == 0
        self.last = lane == latitude - 1
        row = lane.astype(F32)
        self.rot = (time_stride * coriolis / (0.5 * latitude)) * (row - 0.5 * (latitude - 1))

    def up(self, f):
        return jnp.where(self.last, 0.0, pltpu.roll(f, self.n - 1, 1))

    def down(self, f):
        return jnp.where(self.first, 0.0, pltpu.roll(f, 1, 1))

    def diff(self, f):
        return self.up(f) - self.down(f)

    def both(self, f):
        return self.up(f) + self.down(f)


def blocks_of(levels, body):
    lax.fori_loop(0, levels // LB, lambda b, carry: (body(b), carry)[1], 0)


def at(block):
    return pl.ds(pl.multiple_of(block * LB, LB), LB)


def native(block, width):
    size = LB * width
    return pl.ds(pl.multiple_of(block * size, size), size)


def even_tile():
    return lax.axis_index("space") % 2 == 0


def edges(width):
    even = even_tile()
    pair = (jnp.where(even, width - 1, 0), jnp.where(even, width - 2, 1))
    link = (jnp.where(even, 0, width - 1), jnp.where(even, 1, width - 2))
    return pair, link


def halos(width):
    even = even_tile()
    pair = (jnp.where(even, width + 2, 1), jnp.where(even, width + 3, 0))
    link = (jnp.where(even, 1, width + 2), jnp.where(even, 0, width + 3))
    return pair, link


def load_kernel(
    error_hbm, inc_hbm, traj_hbm, mult_hbm, misfit_hbm, land_hbm,
    inc_ref, traj_ref, mult_ref, misfit_ref, land_ref, pair_ref, link_ref, edge_ref, inner_ref, damp_ref,
    error_ref, h_s, sems, small_sems,
):
    subs, fields, width, levels, latitude = inc_ref.shape[0], inc_ref.shape[1], land_ref.shape[0], pair_ref.shape[1], land_ref.shape[1]
    level = lax.broadcasted_iota(jnp.int32, (LB, latitude), 0)

    def copies(b):
        rows = native(b, width)
        first = [
            pltpu.make_async_copy(inc_hbm.at[:, :, rows], inc_ref.at[:, :, rows], sems.at[0, b]),
            pltpu.make_async_copy(traj_hbm.at[:, :, :, rows], traj_ref.at[:, :, :, rows], sems.at[1, b]),
        ]
        second = [
            pltpu.make_async_copy(mult_hbm.at[0, :, rows], mult_ref.at[:, rows], sems.at[2, b]),
            pltpu.make_async_copy(misfit_hbm.at[0, :, rows], misfit_ref.at[:, rows], sems.at[3, b]),
        ]
        return first, second

    land_copy = pltpu.make_async_copy(land_hbm, land_ref, small_sems.at[0])
    error_copy = pltpu.make_async_copy(error_hbm, error_ref, small_sems.at[1])
    for b in range(levels // LB):
        for c in copies(b)[0]:
            c.start()
    land_copy.start()
    error_copy.start()
    for b in range(levels // LB):
        for c in copies(b)[1]:
            c.start()
    land_copy.wait()
    pair_edge, link_edge = edges(width)

    def ahead(b):
        for c in copies(b)[0]:
            c.wait()
        for k in range(subs):
            for j in range(2):
                for s in range(2):
                    h_s[2 * j + s] = traj_ref[k, j, s, native(b, width), :].astype(F32)
            for out, (near, far) in ((pair_ref, pair_edge), (link_ref, link_edge)):
                base = AHEAD * k
                for col, planes, q in ((near, NEAR, QN), (far, FAR, QF)):
                    vals = {f: rows_of(inc_ref, (k, f), b, col, width) for f in planes}
                    for f, p in planes.items():
                        out[base + p, at(b), :] = vals[f].astype(BF16)
                    kt, ks = dens(rows_of(h_s, (0,), 0, col, width), rows_of(h_s, (1,), 0, col, width))
                    out[base + q, at(b), :] = (vals[PR] + gravity * (kt * vals[TE] + ks * vals[SA])).astype(BF16)
                out[base + H0, at(b), :] = rows_of(h_s, (2,), 0, near, width).astype(BF16)
                out[base + H1, at(b), :] = rows_of(h_s, (3,), 0, near, width).astype(BF16)
        for out, (near, _) in ((pair_ref, pair_edge), (link_ref, link_edge)):
            mask = land_ref[pl.ds(near, 1), :].astype(F32)
            out[AHEAD * subs, at(b), :] = jnp.broadcast_to(mask, (LB, mask.shape[1])).astype(BF16)

    def partial(b):
        for f in range(fields):
            damp = jnp.zeros((LB, latitude), F32)
            for i in range(LB):
                damp = jnp.where(level == i, error_ref[f, b * LB + i], damp)
            damp_ref[f, at(b), :] = damp
        for c in copies(b)[1]:
            c.wait()
        for f in range(fields):
            damp = damp_ref[f, at(b), :]
            for c in range(width):
                mult = rows_of(mult_ref, (f,), b, c, width)
                resid = rows_of(misfit_ref, (f,), b, c, width) - damp * mult - rows_of(inc_ref, (0, f), b, c, width)
                value = (mult + relaxation * resid).astype(BF16)
                if 2 <= c < width - 2:
                    inner_ref[f, c - 2, at(b), :] = value
                else:
                    edge_ref[f, c if c < 2 else c - width + 4, at(b), :] = value

    blocks_of(levels, ahead)
    error_copy.wait()
    blocks_of(levels, partial)


def sensor_kernel(
    inc_ref, cell_ref, mult_ref, innov_ref, err_ref, traj_ref, mult_hbm, misfit_hbm,
    obs_ref, spread_ref, sum_ref, dens_ref, mult1_ref, misfit1_ref, hot_s, acc_s, h_s, sems, *, columns,
):
    width, levels = dens_ref.shape[3], dens_ref.shape[4]
    copies = [
        pltpu.make_async_copy(mult_hbm.at[1], mult1_ref, sems.at[0]),
        pltpu.make_async_copy(misfit_hbm.at[1], misfit1_ref, sems.at[1]),
    ]
    for c in copies:
        c.start()

    def density(b):
        for k in range(inc_ref.shape[0]):
            for j in range(2):
                for s in range(2):
                    h_s[s] = traj_ref[k, j, s, native(b, width), :].astype(F32)
                for c in range(width):
                    kt, ks = dens(rows_of(h_s, (0,), 0, c, width), rows_of(h_s, (1,), 0, c, width))
                    dens_ref[k, j, 0, c, at(b), :] = kt
                    dens_ref[k, j, 1, c, at(b), :] = ks

    blocks_of(levels, density)
    subs, rows, latitude = inc_ref.shape[0], 2 * inc_ref.shape[2], inc_ref.shape[3]
    nobs = cell_ref.shape[1]
    share = obs_ref.shape[1]
    blk = 512
    small = 32
    lat_bits = latitude.bit_length() - 1
    col_bits = columns.bit_length() - 1
    offset = lax.axis_index("space") * width
    total = jnp.zeros((1, blk), F32)
    for k in range(subs):
        flat_t = jnp.concatenate([inc_ref[k, 0], inc_ref[k, 1]], axis=0).T
        hi = flat_t.astype(BF16)
        lo = (flat_t - hi.astype(F32)).astype(BF16)
        left = jnp.concatenate([hi, lo], axis=0)
        for b in range(nobs // blk):
            span = slice(b * blk, (b + 1) * blk)
            cell = cell_ref[k : k + 1, span]
            lat = cell & (latitude - 1)
            column = (lax.shift_right_logical(cell, lat_bits) & (columns - 1)) - offset
            owned = (column >= 0) & (column < width)
            row = jnp.where(owned, lax.shift_right_logical(cell, lat_bits + col_bits) * width + column, -1)
            fine = jnp.where(lax.broadcasted_iota(jnp.int32, (small, blk), 0) == (row & (small - 1)), 1.0, 0.0).astype(BF16)
            group = lax.shift_right_arithmetic(row, small.bit_length() - 1)
            for i in range(rows // small):
                coarse = jnp.broadcast_to(jnp.where(group == i, 1.0, 0.0), (small, blk)).astype(BF16)
                hot_s[i * small : (i + 1) * small, :] = coarse * fine
            hot = hot_s[...]
            here = lax.broadcasted_iota(jnp.int32, (latitude, blk), 0) == lat
            both = jnp.dot(left, hot, preferred_element_type=F32)
            seen = jnp.sum(jnp.where(here, both[:latitude] + both[latitude:], 0.0), axis=0, keepdims=True)
            mult = mult_ref[k : k + 1, span]
            resid = innov_ref[k : k + 1, span] - err_ref[k : k + 1, span] * mult - seen
            nxt = mult + relaxation * resid
            total = total + jnp.where(owned, resid * resid, 0.0)
            nhi = nxt.astype(BF16).astype(F32)
            nlo = nxt - nhi
            right = jnp.concatenate([jnp.where(here, nhi, 0.0), jnp.where(here, nlo, 0.0)], axis=0).astype(BF16)
            add = lax.dot_general(hot, right, (((1,), (1,)), ((), ())), preferred_element_type=F32)
            if b == 0:
                acc_s[...] = add
            else:
                acc_s[...] += add
            for i in range(blk // 128):
                g = (k * nobs + b * blk) // 128 + i
                obs_ref[g // share, g % share : g % share + 1, :] = seen[:, i * 128 : (i + 1) * 128]
        spread_ref[k] = acc_s[:, :latitude] + acc_s[:, latitude:]
    sum_ref[...] = total
    for c in copies:
        c.wait()


def team_flags():
    team = lax.axis_index("tm")
    follows = jnp.where(team < lax.axis_size("tm") - 1, 1.0, 0.0).astype(F32)
    return follows, jnp.where(team > 0, 1.0, 0.0).astype(F32)


def forward_kernel(
    inc_ref, dens_ref, land_ref, pair_ref, link_ref, mult_ref, misfit_ref, damp_ref, edge_ref, sensor_ref,
    fwd_ref, send_ref, mult_out, back_pair_ref, back_link_ref, sum_ref, x_s, y_s, q_s, side_s,
):
    subs, fields, width, latitude = inc_ref.shape[0], inc_ref.shape[1], land_ref.shape[0], land_ref.shape[1]
    levels = fwd_ref.shape[2]
    lanes = Rows(latitude)
    keep, _ = team_flags()
    centre = 1.0 - 4.0 * mixing
    even = even_tile()
    pair_halo, link_halo = halos(width)
    sum_ref[...] = jnp.zeros_like(sum_ref)
    sum_ref[0:1, :] = jnp.full((1, latitude), jnp.sum(sensor_ref[...]) / latitude, F32)

    def body(b):
        def beyond(c, plane):
            pair, link = pair_ref[plane, at(b), :].astype(F32), link_ref[plane, at(b), :].astype(F32)
            return jnp.where(even, link, pair) if c < 0 else jnp.where(even, pair, link)

        def mask_at(c):
            if c < 0 or c >= width:
                return beyond(c, AHEAD * subs)
            return jnp.broadcast_to(land_ref[c : c + 1, :].astype(F32), (LB, latitude))

        total = jnp.zeros((LB, latitude), F32)
        for k in reversed(range(subs)):
            base = AHEAD * k
            for c in range(width):
                for f in range(fields):
                    x_s[f, c + 2] = rows_of(inc_ref, (k, f), b, c, width)
                kt, ks = dens_ref[k, 0, 0, c, at(b), :], dens_ref[k, 0, 1, c, at(b), :]
                q_s[c + 2] = x_s[PR, c + 2] + gravity * (kt * x_s[TE, c + 2] + ks * x_s[SA, c + 2])
            for ref, (near, far) in ((pair_ref, pair_halo), (link_ref, link_halo)):
                for f, p in NEAR.items():
                    x_s[f, near] = ref[base + p, at(b), :].astype(F32)
                for f, p in FAR.items():
                    x_s[f, far] = ref[base + p, at(b), :].astype(F32)
                q_s[near] = ref[base + QN, at(b), :].astype(F32)
                q_s[far] = ref[base + QF, at(b), :].astype(F32)

            def substep(src, q, i, mask, with_v):
                te, sa, u, v, pr = (src[f, i] for f in range(5))
                stay, swap = centre * mask, mixing * mask
                thrust = half * mask
                heat = stay * te + swap * (src[TE, i + 1] + src[TE, i - 1] + lanes.both(te))
                salt = stay * sa + swap * (src[SA, i + 1] + src[SA, i - 1] + lanes.both(sa))
                east = mask * (u + lanes.rot * v) - thrust * (q[i + 1] - q[i - 1])
                north = mask * (v - lanes.rot * u) - thrust * lanes.diff(q[i]) if with_v else None
                if mixing == half:
                    around_p = lanes.up(pr - v) + lanes.down(pr + v)
                    around_p = around_p + (src[PR, i + 1] + src[PR, i - 1]) - (src[U, i + 1] - src[U, i - 1])
                    surf = stay * pr + swap * around_p
                else:
                    surf = stay * pr + swap * (src[PR, i + 1] + src[PR, i - 1] + lanes.both(pr))
                    surf = surf - thrust * (src[U, i + 1] - src[U, i - 1] + lanes.diff(v))
                return heat, salt, east, north, surf

            for c in range(-1, width + 1):
                inside = 0 <= c < width
                new = substep(x_s, q_s, c + 2, mask_at(c), inside)
                for f in range(5):
                    if new[f] is not None:
                        y_s[f, c + 2] = new[f]
                if inside:
                    kt, ks = dens_ref[k, 1, 0, c, at(b), :], dens_ref[k, 1, 1, c, at(b), :]
                else:
                    kt, ks = dens(beyond(c, base + H0), beyond(c, base + H1))
                y_s[5, c + 2] = new[PR] + gravity * (kt * new[TE] + ks * new[SA])
            for c in range(width):
                mask = mask_at(c)
                new = substep(y_s, y_s.at[5], c + 2, mask, True)
                for f in range(fields):
                    if k == subs - 1:
                        fwd_ref[f, c, at(b), :] = new[f]
                        send_ref[f, c, at(b), :] = new[f].astype(BF16)
                        if c < 2 or c >= width - 2:
                            got = edge_ref[f, c if c < 2 else c - width + 4, at(b), :].astype(F32)
                            after = mask * (keep * (got + relaxation * new[f]))
                    else:
                        mult = rows_of(mult_ref, (f,), b, c, width)
                        resid = (
                            rows_of(misfit_ref, (f,), b, c, width)
                            - damp_ref[f, at(b), :] * mult
                            - (rows_of(inc_ref, (k + 1, f), b, c, width) - new[f])
                        )
                        total = total + resid * resid
                        after = mult + relaxation * resid
                        mult_out[f, c, at(b), :] = after
                        after = mask * after
                    where = BACK * k
                    if c == width - 1:
                        side_s[1, where + NEAR[f]] = after
                    if c == width - 2 and f != V:
                        side_s[1, where + FAR[f]] = after
                    if c == 0:
                        side_s[0, where + NEAR[f]] = after
                    if c == 1 and f != V:
                        side_s[0, where + FAR[f]] = after
        up = jnp.where(even, 1, 0)
        for p in range(BACK * subs):
            back_pair_ref[p, at(b), :] = side_s[up, p].astype(BF16)
            back_link_ref[p, at(b), :] = side_s[1 - up, p].astype(BF16)
        sum_ref[...] += total

    blocks_of(levels, body)


def adjoint_kernel(
    inc_ref, dens_ref, land_ref, pair_ref, link_ref, back_pair_ref, back_link_ref, mult_ref, misfit_ref, damp_ref,
    fwd_ref, mnext_ref, edge_ref, inner_ref, prev_ref, spread_ref, sum_ref, seen_ref,
    mult_out, grad_ref, fin_ref, x_s, y_s, acc_s,
):
    subs, fields, width, latitude = dens_ref.shape[0], mult_ref.shape[0], land_ref.shape[0], land_ref.shape[1]
    lanes = Rows(latitude)
    keep, precede = team_flags()
    centre = 1.0 - 4.0 * mixing
    even = even_tile()
    pair_halo, link_halo = halos(width)
    b = pl.program_id(0)

    @pl.when(b == 0)
    def _():
        acc_s[...] = jnp.zeros_like(acc_s)

    def body():
        def beyond(c, plane):
            pair, link = pair_ref[plane, at(b), :].astype(F32), link_ref[plane, at(b), :].astype(F32)
            return jnp.where(even, link, pair) if c < 0 else jnp.where(even, pair, link)

        def mask_at(c):
            if c < 0 or c >= width:
                return beyond(c, AHEAD * subs)
            return jnp.broadcast_to(land_ref[c : c + 1, :].astype(F32), (LB, latitude))

        misfit_total = jnp.zeros((LB, latitude), F32)
        grad_total = jnp.zeros((LB, latitude), F32)
        for k in range(subs):
            for c in range(width):
                mask = mask_at(c)
                for f in range(fields):
                    if k == subs - 1:
                        if 2 <= c < width - 2:
                            got = inner_ref[f, c - 2, at(b), :]
                        else:
                            got = edge_ref[f, c if c < 2 else c - width + 4, at(b), :]
                        value = keep * (got.astype(F32) + relaxation * fwd_ref[f, c, at(b), :])
                    else:
                        value = mnext_ref[f, c, at(b), :]
                    x_s[f, c + 2] = mask * value
            for ref, (near, far) in ((back_pair_ref, pair_halo), (back_link_ref, link_halo)):
                for f, p in NEAR.items():
                    x_s[f, near] = ref[BACK * k + p, at(b), :].astype(F32)
                for f, p in FAR.items():
                    x_s[f, far] = ref[BACK * k + p, at(b), :].astype(F32)

            def back(src, i, kt, ks, with_v):
                te, sa, u, v, pr = (src[f, i] for f in range(5))
                mix = lambda f, x: centre * x + mixing * (src[f, i + 1] + src[f, i - 1] + lanes.both(x))
                q = half * (src[U, i + 1] - src[U, i - 1] + lanes.diff(v))
                gq = gravity * q if gravity != 1.0 else q
                heat = mix(TE, te) + kt * gq
                salt = mix(SA, sa) + ks * gq
                east = u - lanes.rot * v + half * (src[PR, i + 1] - src[PR, i - 1])
                north = v + lanes.rot * u + half * lanes.diff(pr) if with_v else None
                surf = mix(PR, pr) + q
                return heat, salt, east, north, surf

            for c in range(-1, width + 1):
                inside = 0 <= c < width
                if inside:
                    kt, ks = dens_ref[k, 1, 0, c, at(b), :], dens_ref[k, 1, 1, c, at(b), :]
                else:
                    kt, ks = dens(beyond(c, AHEAD * k + H0), beyond(c, AHEAD * k + H1))
                mask = mask_at(c)
                new = back(x_s, c + 2, kt, ks, inside)
                for f in range(5):
                    if new[f] is not None:
                        y_s[f, c + 2] = mask * new[f]
            for c in range(width):
                new = back(y_s, c + 2, dens_ref[k, 0, 0, c, at(b), :], dens_ref[k, 0, 1, c, at(b), :], True)
                for f in range(fields):
                    if k == 0:
                        mult = rows_of(mult_ref, (f,), b, c, width)
                        resid = (
                            rows_of(misfit_ref, (f,), b, c, width)
                            - damp_ref[f, at(b), :] * mult
                            - (rows_of(inc_ref, (0, f), b, c, width) - precede * prev_ref[f, c, at(b), :].astype(F32))
                        )
                        misfit_total = misfit_total + resid * resid
                        value = mult + relaxation * resid
                    else:
                        value = mnext_ref[f, c, at(b), :]
                    spot = pl.ds(b * (LB * width) + c, LB, stride=width)
                    mult_out[k, f, pl.ds(c, LB, stride=width), :] = value
                    grad = value - new[f]
                    if f < 2:
                        grad = grad + rows_of(spread_ref, (k, f), b, c, width)
                    grad_total = grad_total + grad * grad
                    grad_ref[k, f, spot, :] = grad
        acc_s[0] += misfit_total
        acc_s[1] += grad_total

    body()

    @pl.when(b == pl.num_programs(0) - 1)
    def _():
        misfit_sum = jnp.sum(acc_s[0] + sum_ref[...])
        grad_sum = jnp.sum(acc_s[1])
        lane = lax.broadcasted_iota(jnp.int32, (1, 128), 1)
        scalars = jnp.where(lane == 0, misfit_sum, jnp.where(lane == 1, grad_sum, 0.0))
        pieces = jnp.sum(seen_ref[...], axis=0)
        peers = fin_ref.shape[0]
        for i in range(peers):
            fin_ref[i, 0:1, :] = scalars
            fin_ref[i, 1:, :] = pieces


def step_kernel(recv_ref, inc_ref, grad_ref, mult_ref, innov_ref, err_ref, out_ref, next_ref):
    parts = recv_ref[:, 0, :]
    sums = jnp.sum(parts, axis=0, keepdims=True)
    lane = lax.broadcasted_iota(jnp.int32, sums.shape, 1)
    misfit_square = jnp.sum(jnp.where(lane == 0, sums, 0.0), axis=1, keepdims=True)
    gradient_square = jnp.sum(jnp.where(lane == 1, sums, 0.0), axis=1, keepdims=True)
    stride = misfit_square / (gradient_square + epsilon)
    size = out_ref.shape[2]
    b = pl.program_id(0)
    spot = pl.ds(pl.multiple_of(b * size, size), size)
    for k in range(inc_ref.shape[0]):
        for f in range(inc_ref.shape[1]):
            out_ref[k, f] = inc_ref[k, f, spot, :] - stride * grad_ref[k, f, spot, :]

    @pl.when(b == 0)
    def _():
        subs, nobs = mult_ref.shape
        share = recv_ref.shape[1] - 1
        first = lax.axis_index("tm") * lax.axis_size("space")
        for k in range(subs):
            for i in range(nobs // 128):
                g = k * (nobs // 128) + i
                span = slice(i * 128, (i + 1) * 128)
                seen = recv_ref[first + g // share, 1 + g % share : 2 + g % share, :]
                mult = mult_ref[k : k + 1, span]
                resid = innov_ref[k : k + 1, span] - err_ref[k : k + 1, span] * mult - seen
                next_ref[k : k + 1, span] = mult + relaxation * resid


def shifted(shard, axis, by):
    peers = lax.axis_size(axis)
    return lax.ppermute(shard, axis, [(i, (i + by) % peers) for i in range(peers)])


def swapped(shard, axis, pair):
    peers = lax.axis_size(axis)
    ahead = 0 if pair else 1
    return lax.ppermute(shard, axis, [(i, (i + (1 if i % 2 == ahead else -1)) % peers) for i in range(peers)])


def within(
    increment, multiplier, sensor_multiplier, misfit, innovation,
    model_error, sensor_error, trajectory, land_sea, sensor_cells,
):
    subs, fields, levels, width, latitude = increment.shape
    nobs = sensor_cells.shape[1]
    teams, tiles = lax.axis_size("tm"), lax.axis_size("space")
    peers = teams * tiles
    share = subs * nobs // (128 * tiles)
    assert tiles % 2 == 0 and fields == 5 and trajectory.shape[1] == 2 and subs == 2 and levels % LB == 0 and width >= 4
    assert latitude == 128 and (width * tiles) & (width * tiles - 1) == 0 and nobs % 512 == 0
    assert share * 128 * tiles == subs * nobs and (2 * levels * width) % 32 == 0
    rows = levels * width
    fast = lambda x: pltpu.with_memory_space_constraint(x, pltpu.VMEM)
    slow = lambda x: pltpu.with_memory_space_constraint(x, pltpu.HBM)
    native_shape = (subs, fields, rows, latitude)
    inc = slow(increment.reshape(native_shape))
    traj = slow(trajectory.reshape(subs, 2, 2, rows, latitude))
    mult = slow(multiplier.reshape(native_shape))
    mis = slow(misfit.reshape(native_shape))
    cells, sen_m, sen_i, sen_e = (fast(x) for x in (sensor_cells, sensor_multiplier, innovation, sensor_error))
    vmem = pl.BlockSpec(memory_space=pltpu.VMEM)
    hbm = pl.BlockSpec(memory_space=pltpu.HBM)
    scr = lambda *s: pltpu.VMEM(s, F32)
    limit = pltpu.CompilerParams(vmem_limit_bytes=VMEM_LIMIT)

    def call(kernel, outs, scratch, *args, specs=None):
        return pl.pallas_call(
            kernel,
            in_specs=specs or [vmem] * len(args),
            out_specs=[vmem] * len(outs),
            out_shape=[pltpu.VMEM(s, d) for s, d in outs],
            scratch_shapes=scratch,
            compiler_params=limit,
        )(*args)

    ahead = (subs * AHEAD + 1, levels, latitude)
    one = native_shape[1:]
    inc, traj, mult0, mis0, land, pair, link, edge, inner, damp = call(
        load_kernel,
        [
            (native_shape, F32), (traj.shape, BF16), (one, F32), (one, F32), (land_sea.shape, jnp.int32),
            (ahead, BF16), (ahead, BF16),
            ((fields, 4, levels, latitude), BF16),
            ((fields, width - 4, levels, latitude), BF16),
            ((fields, levels, latitude), F32),
        ],
        [
            pltpu.SMEM(model_error.shape, F32), scr(4, LB * width, latitude),
            pltpu.SemaphoreType.DMA((4, levels // LB)), pltpu.SemaphoreType.DMA((2,)),
        ],
        slow(model_error), inc, traj, mult, mis, slow(land_sea),
        specs=[hbm] * 6,
    )
    link_in = fast(swapped(link, "space", False))
    pair_in = fast(swapped(pair, "space", True))
    edge_in = fast(shifted(edge, "tm", -1))
    inner_in = fast(shifted(inner, "tm", -1))

    seen, spread, sensor_sum, density, mult1, mis1 = call(
        lambda *refs: sensor_kernel(*refs, columns=width * tiles),
        [
            ((tiles, share, 128), F32), ((subs, 2 * rows, latitude), F32), ((1, 512), F32),
            ((subs, 2, 2, width, levels, latitude), F32), (one, F32), (one, F32),
        ],
        [
            pltpu.VMEM((2 * rows, 512), BF16), scr(2 * rows, 2 * latitude), scr(2, LB * width, latitude),
            pltpu.SemaphoreType.DMA((2,)),
        ],
        inc, cells, sen_m, sen_i, sen_e, traj, mult, mis,
        specs=[vmem] * 6 + [hbm] * 2,
    )
    spread = spread.reshape(subs, 2, rows, latitude)
    seen_in = fast(lax.all_to_all(seen, "space", 0, 0))

    column = (fields, width, levels, latitude)
    behind = (subs * BACK, levels, latitude)
    fwd, send, mnext, back_pair, back_link, sums = call(
        forward_kernel,
        [(column, F32), (column, BF16), (column, F32), (behind, BF16), (behind, BF16), ((LB, latitude), F32)],
        [
            scr(5, width + 4, LB, latitude), scr(6, width + 4, LB, latitude), scr(width + 4, LB, latitude),
            scr(2, subs * BACK, LB, latitude),
        ],
        inc, density, land, pair_in, link_in, mult1, mis1, damp, edge_in, sensor_sum,
    )
    back_link_in = fast(swapped(back_link, "space", False))
    back_pair_in = fast(swapped(back_pair, "space", True))
    prev = fast(shifted(send, "tm", 1))

    block = pl.BlockSpec((subs, fields, LB * width, latitude), lambda i: (0, 0, i, 0))
    mult_next, gradient, final = pl.pallas_call(
        adjoint_kernel,
        name="adjoint",
        grid=(levels // LB,),
        in_specs=[vmem] * 18,
        out_specs=[block, vmem, vmem],
        out_shape=[
            jax.ShapeDtypeStruct(native_shape, F32),
            pltpu.VMEM(native_shape, F32),
            pltpu.VMEM((peers, 1 + share, 128), F32),
        ],
        scratch_shapes=[scr(5, width + 4, LB, latitude), scr(5, width + 4, LB, latitude), scr(2, LB, latitude)],
        compiler_params=limit,
    )(
        inc, density, land, pair_in, link_in, back_pair_in, back_link_in, mult0, mis0, damp,
        fwd, mnext, edge_in, inner_in, prev, spread, sums, seen_in,
    )
    final = fast(lax.all_to_all(final, ("tm", "space"), 0, 0))

    steps = 4 if rows % 32 == 0 else 1
    size = rows // steps
    increment_next, sensor_next = pl.pallas_call(
        lambda *refs: step_kernel(*refs),
        name="step",
        grid=(steps,),
        in_specs=[vmem] * 6,
        out_specs=[
            pl.BlockSpec((subs, fields, size, latitude), lambda i: (0, 0, i, 0)),
            pl.BlockSpec((subs, nobs), lambda i: (0, 0)),
        ],
        out_shape=[
            jax.ShapeDtypeStruct(native_shape, F32),
            jax.ShapeDtypeStruct((subs, nobs), F32),
        ],
        compiler_params=limit,
    )(final, inc, gradient, sen_m, sen_i, sen_e)
    return (increment_next.reshape(increment.shape), mult_next.reshape(multiplier.shape), sensor_next)


def solution(mesh):
    state = P("tm", None, None, "space", None)
    placed = (
        state,
        state,
        P("tm", None),
        state,
        P("tm", None),
        P(),
        P("tm", None),
        P("tm", None, None, None, "space", None),
        P("space", None),
        P("tm", None),
    )
    return jax.shard_map(
        within,
        mesh=mesh,
        in_specs=placed,
        out_specs=(state, state, P("tm", None)),
        check_vma=False,
    )
```

```python
import jax
import jax.numpy as jnp
from jax import lax
from jax.experimental import pallas as pl
from jax.experimental.pallas import tpu as pltpu
from jax.sharding import PartitionSpec as P


thermal_lin = 0.2
thermal_quad = 0.02
haline_lin = 0.8
cabbeling = 0.01
gravity = 1.0
time_stride = 0.3
mixing = 0.15
coriolis = 0.5
relaxation = 0.5
epsilon = 1e-06

kt0 = -thermal_lin + 10.0 * thermal_quad - 5.0 * cabbeling
kt1 = -30.0 * thermal_quad
kt2 = 8.0 * cabbeling
ks0 = haline_lin - 10.0 * cabbeling
ks1 = 30.0 * cabbeling
half = 0.5 * time_stride

LB = 16
VMEM_LIMIT = 24 * 1024 * 1024
SCATTER_ROWS = 256
TE, SA, U, V, PR = range(5)
F32 = jnp.float32
BF16 = jnp.bfloat16

NEAR = {TE: 0, SA: 1, U: 2, V: 3, PR: 4}
FAR = {TE: 5, SA: 6, U: 7, PR: 8}
BACK = 9
QN, QF, H0, H1 = 9, 10, 11, 12
AHEAD = 13


def rows_of(ref, lead, block, col, width):
    return ref[lead + (pl.ds(block * (LB * width) + col, LB, stride=width), slice(None))]


def dens(h0, h1):
    return kt0 + kt1 * h0 + kt2 * h1, ks0 + ks1 * h0


class Rows:
    def __init__(self, latitude):
        lane = lax.broadcasted_iota(jnp.int32, (LB, latitude), 1)
        self.n = latitude
        self.first = lane == 0
        self.last = lane == latitude - 1
        row = lane.astype(F32)
        self.rot = (time_stride * coriolis / (0.5 * latitude)) * (row - 0.5 * (latitude - 1))

    def up(self, f):
        return jnp.where(self.last, 0.0, pltpu.roll(f, self.n - 1, 1))

    def down(self, f):
        return jnp.where(self.first, 0.0, pltpu.roll(f, 1, 1))

    def diff(self, f):
        return self.up(f) - self.down(f)

    def both(self, f):
        return self.up(f) + self.down(f)


def blocks_of(levels, body):
    lax.fori_loop(0, levels // LB, lambda b, carry: (body(b), carry)[1], 0)


def at(block):
    return pl.ds(pl.multiple_of(block * LB, LB), LB)


def native(block, width):
    size = LB * width
    return pl.ds(pl.multiple_of(block * size, size), size)


def even_tile():
    return lax.axis_index("space") % 2 == 0


def edges(width):
    even = even_tile()
    pair = (jnp.where(even, width - 1, 0), jnp.where(even, width - 2, 1))
    link = (jnp.where(even, 0, width - 1), jnp.where(even, 1, width - 2))
    return pair, link


def halos(width):
    even = even_tile()
    pair = (jnp.where(even, width + 2, 1), jnp.where(even, width + 3, 0))
    link = (jnp.where(even, 1, width + 2), jnp.where(even, 0, width + 3))
    return pair, link


def load_kernel(
    error_hbm, inc_hbm, traj_hbm, mult_hbm, misfit_hbm, land_hbm,
    inc_ref, traj_ref, mult_ref, misfit_ref, land_ref, pair_ref, link_ref, edge_ref, inner_ref, damp_ref,
    error_ref, h_s, sems, small_sems,
):
    subs, fields, width, levels, latitude = inc_ref.shape[0], inc_ref.shape[1], land_ref.shape[0], pair_ref.shape[1], land_ref.shape[1]
    level = lax.broadcasted_iota(jnp.int32, (LB, latitude), 0)

    def copies(b):
        rows = native(b, width)
        first = [
            pltpu.make_async_copy(inc_hbm.at[:, :, rows], inc_ref.at[:, :, rows], sems.at[0, b]),
            pltpu.make_async_copy(traj_hbm.at[:, :, :, rows], traj_ref.at[:, :, :, rows], sems.at[1, b]),
        ]
        second = [
            pltpu.make_async_copy(mult_hbm.at[0, :, rows], mult_ref.at[:, rows], sems.at[2, b]),
            pltpu.make_async_copy(misfit_hbm.at[0, :, rows], misfit_ref.at[:, rows], sems.at[3, b]),
        ]
        return first, second

    land_copy = pltpu.make_async_copy(land_hbm, land_ref, small_sems.at[0])
    error_copy = pltpu.make_async_copy(error_hbm, error_ref, small_sems.at[1])
    for b in range(levels // LB):
        for c in copies(b)[0]:
            c.start()
    land_copy.start()
    error_copy.start()
    for b in range(levels // LB):
        for c in copies(b)[1]:
            c.start()
    land_copy.wait()
    pair_edge, link_edge = edges(width)

    def ahead(b):
        for c in copies(b)[0]:
            c.wait()
        for k in range(subs):
            for j in range(2):
                for s in range(2):
                    h_s[2 * j + s] = traj_ref[k, j, s, native(b, width), :].astype(F32)
            for out, (near, far) in ((pair_ref, pair_edge), (link_ref, link_edge)):
                base = AHEAD * k
                for col, planes, q in ((near, NEAR, QN), (far, FAR, QF)):
                    vals = {f: rows_of(inc_ref, (k, f), b, col, width) for f in planes}
                    for f, p in planes.items():
                        out[base + p, at(b), :] = vals[f].astype(BF16)
                    kt, ks = dens(rows_of(h_s, (0,), 0, col, width), rows_of(h_s, (1,), 0, col, width))
                    out[base + q, at(b), :] = (vals[PR] + gravity * (kt * vals[TE] + ks * vals[SA])).astype(BF16)
                out[base + H0, at(b), :] = rows_of(h_s, (2,), 0, near, width).astype(BF16)
                out[base + H1, at(b), :] = rows_of(h_s, (3,), 0, near, width).astype(BF16)
        for out, (near, _) in ((pair_ref, pair_edge), (link_ref, link_edge)):
            mask = land_ref[pl.ds(near, 1), :].astype(F32)
            out[AHEAD * subs, at(b), :] = jnp.broadcast_to(mask, (LB, mask.shape[1])).astype(BF16)

    def partial(b):
        for f in range(fields):
            damp = jnp.zeros((LB, latitude), F32)
            for i in range(LB):
                damp = jnp.where(level == i, error_ref[f, b * LB + i], damp)
            damp_ref[f, at(b), :] = damp
        for c in copies(b)[1]:
            c.wait()
        for f in range(fields):
            damp = damp_ref[f, at(b), :]
            for c in range(width):
                mult = rows_of(mult_ref, (f,), b, c, width)
                resid = rows_of(misfit_ref, (f,), b, c, width) - damp * mult - rows_of(inc_ref, (0, f), b, c, width)
                value = (mult + relaxation * resid).astype(BF16)
                if 2 <= c < width - 2:
                    inner_ref[f, c - 2, at(b), :] = value
                else:
                    edge_ref[f, c if c < 2 else c - width + 4, at(b), :] = value

    blocks_of(levels, ahead)
    error_copy.wait()
    blocks_of(levels, partial)


def sensor_kernel(
    inc_ref, cell_ref, mult_ref, innov_ref, err_ref, traj_ref, mult_hbm, misfit_hbm,
    obs_ref, spread_ref, sum_ref, dens_ref, mult1_ref, misfit1_ref, hot_s, right_s, h_s, sems, *, columns,
):
    width, levels = dens_ref.shape[3], dens_ref.shape[4]
    copies = [
        pltpu.make_async_copy(mult_hbm.at[1], mult1_ref, sems.at[0]),
        pltpu.make_async_copy(misfit_hbm.at[1], misfit1_ref, sems.at[1]),
    ]
    for c in copies:
        c.start()

    def density(b):
        for k in range(inc_ref.shape[0]):
            for j in range(2):
                for s in range(2):
                    h_s[s] = traj_ref[k, j, s, native(b, width), :].astype(F32)
                for c in range(width):
                    kt, ks = dens(rows_of(h_s, (0,), 0, c, width), rows_of(h_s, (1,), 0, c, width))
                    dens_ref[k, j, 0, c, at(b), :] = kt
                    dens_ref[k, j, 1, c, at(b), :] = ks

    blocks_of(levels, density)
    subs, rows, latitude = inc_ref.shape[0], 2 * inc_ref.shape[2], inc_ref.shape[3]
    nobs = cell_ref.shape[1]
    share = obs_ref.shape[1]
    blk = 512
    small = 32
    lat_bits = latitude.bit_length() - 1
    col_bits = columns.bit_length() - 1
    offset = lax.axis_index("space") * width
    total = jnp.zeros((1, blk), F32)
    for k in range(subs):
        flat_t = jnp.concatenate([inc_ref[k, 0], inc_ref[k, 1]], axis=0).T
        hi = flat_t.astype(BF16)
        lo = (flat_t - hi.astype(F32)).astype(BF16)
        left = jnp.concatenate([hi, lo], axis=0)
        for b in range(nobs // blk):
            span = slice(b * blk, (b + 1) * blk)
            cell = cell_ref[k : k + 1, span]
            lat = cell & (latitude - 1)
            column = (lax.shift_right_logical(cell, lat_bits) & (columns - 1)) - offset
            owned = (column >= 0) & (column < width)
            row = jnp.where(owned, lax.shift_right_logical(cell, lat_bits + col_bits) * width + column, -1)
            fine = jnp.where(lax.broadcasted_iota(jnp.int32, (small, blk), 0) == (row & (small - 1)), 1.0, 0.0).astype(BF16)
            group = lax.shift_right_arithmetic(row, small.bit_length() - 1)
            for i in range(rows // small):
                coarse = jnp.broadcast_to(jnp.where(group == i, 1.0, 0.0), (small, blk)).astype(BF16)
                hot_s[i * small : (i + 1) * small, span] = coarse * fine
            hot = hot_s[:, span]
            here = lax.broadcasted_iota(jnp.int32, (latitude, blk), 0) == lat
            both = jnp.dot(left, hot, preferred_element_type=F32)
            seen = jnp.sum(jnp.where(here, both[:latitude] + both[latitude:], 0.0), axis=0, keepdims=True)
            mult = mult_ref[k : k + 1, span]
            resid = innov_ref[k : k + 1, span] - err_ref[k : k + 1, span] * mult - seen
            nxt = mult + relaxation * resid
            total = total + jnp.where(owned, resid * resid, 0.0)
            nhi = nxt.astype(BF16).astype(F32)
            nlo = nxt - nhi
            right_s[:latitude, span] = jnp.where(here, nhi, 0.0).astype(BF16)
            right_s[latitude:, span] = jnp.where(here, nlo, 0.0).astype(BF16)
            for i in range(blk // 128):
                g = (k * nobs + b * blk) // 128 + i
                obs_ref[g // share, g % share : g % share + 1, :] = seen[:, i * 128 : (i + 1) * 128]
        part = SCATTER_ROWS if rows % SCATTER_ROWS == 0 else rows
        for r in range(rows // part):
            here = slice(r * part, (r + 1) * part)
            both = lax.dot_general(hot_s[here, :], right_s[...], (((1,), (1,)), ((), ())), preferred_element_type=F32)
            spread_ref[k, here, :] = both[:, :latitude] + both[:, latitude:]
    sum_ref[...] = total
    for c in copies:
        c.wait()


def team_flags():
    team = lax.axis_index("tm")
    follows = jnp.where(team < lax.axis_size("tm") - 1, 1.0, 0.0).astype(F32)
    return follows, jnp.where(team > 0, 1.0, 0.0).astype(F32)


def tangent(lanes, src, q, i, mask, with_v):
    te, sa, u, v, pr = (src[f, i] for f in range(5))
    stay, swap, thrust = (1.0 - 4.0 * mixing) * mask, mixing * mask, half * mask
    heat = stay * te + swap * (src[TE, i + 1] + src[TE, i - 1] + lanes.both(te))
    salt = stay * sa + swap * (src[SA, i + 1] + src[SA, i - 1] + lanes.both(sa))
    east = mask * (u + lanes.rot * v) - thrust * (q[i + 1] - q[i - 1])
    north = mask * (v - lanes.rot * u) - thrust * lanes.diff(q[i]) if with_v else None
    if mixing == half:
        around_p = lanes.up(pr - v) + lanes.down(pr + v)
        around_p = around_p + (src[PR, i + 1] + src[PR, i - 1]) - (src[U, i + 1] - src[U, i - 1])
        surf = stay * pr + swap * around_p
    else:
        surf = stay * pr + swap * (src[PR, i + 1] + src[PR, i - 1] + lanes.both(pr))
        surf = surf - thrust * (src[U, i + 1] - src[U, i - 1] + lanes.diff(v))
    return heat, salt, east, north, surf


def fill(inc_ref, dens_ref, x_s, q_s, k, b, c, width):
    for f in range(5):
        x_s[f, c + 2] = rows_of(inc_ref, (k, f), b, c, width)
    kt, ks = dens_ref[k, 0, 0, c, at(b), :], dens_ref[k, 0, 1, c, at(b), :]
    q_s[c + 2] = x_s[PR, c + 2] + gravity * (kt * x_s[TE, c + 2] + ks * x_s[SA, c + 2])


def renew(inc_ref, mult_ref, misfit_ref, damp_ref, new, f, b, c, width):
    mult = rows_of(mult_ref, (f,), b, c, width)
    resid = (
        rows_of(misfit_ref, (f,), b, c, width)
        - damp_ref[f, at(b), :] * mult
        - (rows_of(inc_ref, (1, f), b, c, width) - new)
    )
    return mult + relaxation * resid, resid


def interior_kernel(
    inc_ref, dens_ref, land_ref, mult_ref, misfit_ref, damp_ref, sensor_ref,
    mid_ref, fwd_ref, send_ref, mult_out, sum_ref, x_s, y_s, q_s,
):
    subs, fields, width, latitude = inc_ref.shape[0], inc_ref.shape[1], land_ref.shape[0], land_ref.shape[1]
    levels = fwd_ref.shape[2]
    lanes = Rows(latitude)
    sum_ref[...] = jnp.zeros_like(sum_ref)
    sum_ref[0:1, :] = jnp.full((1, latitude), jnp.sum(sensor_ref[...]) / latitude, F32)

    def body(b):
        mask_at = lambda c: jnp.broadcast_to(land_ref[c : c + 1, :].astype(F32), (LB, latitude))
        total = jnp.zeros((LB, latitude), F32)
        for k in reversed(range(subs)):
            for c in range(width):
                fill(inc_ref, dens_ref, x_s, q_s, k, b, c, width)
            for c in range(1, width - 1):
                new = tangent(lanes, x_s, q_s, c + 2, mask_at(c), True)
                kt, ks = dens_ref[k, 1, 0, c, at(b), :], dens_ref[k, 1, 1, c, at(b), :]
                new = new + (new[PR] + gravity * (kt * new[TE] + ks * new[SA]),)
                for f in range(6):
                    y_s[f, c + 2] = new[f]
                    if c in (1, 2):
                        mid_ref[k, f, c - 1, at(b), :] = new[f]
                    if c in (width - 3, width - 2):
                        mid_ref[k, f, c - width + 5, at(b), :] = new[f]
            for c in range(2, width - 2):
                new = tangent(lanes, y_s, y_s.at[5], c + 2, mask_at(c), True)
                for f in range(fields):
                    if k == 1:
                        fwd_ref[f, c - 2, at(b), :] = new[f]
                        send_ref[f, c - 2, at(b), :] = new[f].astype(BF16)
                    else:
                        value, resid = renew(inc_ref, mult_ref, misfit_ref, damp_ref, new[f], f, b, c, width)
                        total = total + resid * resid
                        mult_out[f, c - 2, at(b), :] = value
        sum_ref[...] += total

    blocks_of(levels, body)


def edge_kernel(
    inc_ref, dens_ref, land_ref, pair_ref, link_ref, mult_ref, misfit_ref, damp_ref, edge_ref, mid_ref, part_ref,
    fwd_ref, send_ref, mult_out, back_pair_ref, back_link_ref, sum_ref, x_s, y_s, q_s, side_s,
):
    subs, fields, width, latitude = inc_ref.shape[0], inc_ref.shape[1], land_ref.shape[0], land_ref.shape[1]
    levels = fwd_ref.shape[2]
    lanes = Rows(latitude)
    keep, _ = team_flags()
    even = even_tile()
    pair_halo, link_halo = halos(width)
    outer = (0, 1, width - 2, width - 1)
    sum_ref[...] = part_ref[...]

    def body(b):
        def beyond(c, plane):
            pair, link = pair_ref[plane, at(b), :].astype(F32), link_ref[plane, at(b), :].astype(F32)
            return jnp.where(even, link, pair) if c < 0 else jnp.where(even, pair, link)

        def mask_at(c):
            if c < 0 or c >= width:
                return beyond(c, AHEAD * subs)
            return jnp.broadcast_to(land_ref[c : c + 1, :].astype(F32), (LB, latitude))

        total = jnp.zeros((LB, latitude), F32)
        for k in reversed(range(subs)):
            base = AHEAD * k
            for c in outer:
                fill(inc_ref, dens_ref, x_s, q_s, k, b, c, width)
            for ref, (near, far) in ((pair_ref, pair_halo), (link_ref, link_halo)):
                for f, p in NEAR.items():
                    x_s[f, near] = ref[base + p, at(b), :].astype(F32)
                for f, p in FAR.items():
                    x_s[f, far] = ref[base + p, at(b), :].astype(F32)
                q_s[near] = ref[base + QN, at(b), :].astype(F32)
                q_s[far] = ref[base + QF, at(b), :].astype(F32)
            for i, c in enumerate((1, 2, width - 3, width - 2)):
                for f in range(6):
                    y_s[f, c + 2] = mid_ref[k, f, i, at(b), :]
            for c in (-1, 0, width - 1, width):
                inside = 0 <= c < width
                new = tangent(lanes, x_s, q_s, c + 2, mask_at(c), inside)
                for f in range(5):
                    if new[f] is not None:
                        y_s[f, c + 2] = new[f]
                if inside:
                    kt, ks = dens_ref[k, 1, 0, c, at(b), :], dens_ref[k, 1, 1, c, at(b), :]
                else:
                    kt, ks = dens(beyond(c, base + H0), beyond(c, base + H1))
                y_s[5, c + 2] = new[PR] + gravity * (kt * new[TE] + ks * new[SA])
            for i, c in enumerate(outer):
                mask = mask_at(c)
                new = tangent(lanes, y_s, y_s.at[5], c + 2, mask, True)
                for f in range(fields):
                    if k == 1:
                        fwd_ref[f, i, at(b), :] = new[f]
                        send_ref[f, i, at(b), :] = new[f].astype(BF16)
                        got = edge_ref[f, i, at(b), :].astype(F32)
                        after = mask * (keep * (got + relaxation * new[f]))
                    else:
                        value, resid = renew(inc_ref, mult_ref, misfit_ref, damp_ref, new[f], f, b, c, width)
                        total = total + resid * resid
                        mult_out[f, i, at(b), :] = value
                        after = mask * value
                    plane = NEAR[f] if i in (0, 3) else FAR.get(f)
                    if plane is not None:
                        side_s[i // 2, BACK * k + plane] = after
        up = jnp.where(even, 1, 0)
        for p in range(BACK * subs):
            back_pair_ref[p, at(b), :] = side_s[up, p].astype(BF16)
            back_link_ref[p, at(b), :] = side_s[1 - up, p].astype(BF16)
        sum_ref[...] += total

    blocks_of(levels, body)


def column_of(inner_ref, outer_ref, f, b, c, width):
    if 2 <= c < width - 2:
        return inner_ref[f, c - 2, at(b), :]
    return outer_ref[f, c if c < 2 else c - width + 4, at(b), :]


def adjoint_kernel(
    inc_ref, dens_ref, land_ref, pair_ref, link_ref, back_pair_ref, back_link_ref, mult_ref, misfit_ref, damp_ref,
    fwd_in, fwd_out, mnext_in, mnext_out, edge_ref, inner_ref, prev_in, prev_out, spread_ref, sum_ref, seen_ref,
    mult_out, grad_ref, fin_ref, x_s, y_s, acc_s,
):
    subs, fields, width, latitude = dens_ref.shape[0], mult_ref.shape[0], land_ref.shape[0], land_ref.shape[1]
    lanes = Rows(latitude)
    keep, precede = team_flags()
    centre = 1.0 - 4.0 * mixing
    even = even_tile()
    pair_halo, link_halo = halos(width)
    b = pl.program_id(0)

    @pl.when(b == 0)
    def _():
        acc_s[...] = jnp.zeros_like(acc_s)

    def body():
        def beyond(c, plane):
            pair, link = pair_ref[plane, at(b), :].astype(F32), link_ref[plane, at(b), :].astype(F32)
            return jnp.where(even, link, pair) if c < 0 else jnp.where(even, pair, link)

        def mask_at(c):
            if c < 0 or c >= width:
                return beyond(c, AHEAD * subs)
            return jnp.broadcast_to(land_ref[c : c + 1, :].astype(F32), (LB, latitude))

        misfit_total = jnp.zeros((LB, latitude), F32)
        grad_total = jnp.zeros((LB, latitude), F32)
        for k in range(subs):
            for c in range(width):
                mask = mask_at(c)
                for f in range(fields):
                    if k == subs - 1:
                        got = column_of(inner_ref, edge_ref, f, b, c, width).astype(F32)
                        value = keep * (got + relaxation * column_of(fwd_in, fwd_out, f, b, c, width))
                    else:
                        value = column_of(mnext_in, mnext_out, f, b, c, width)
                    x_s[f, c + 2] = mask * value
            for ref, (near, far) in ((back_pair_ref, pair_halo), (back_link_ref, link_halo)):
                for f, p in NEAR.items():
                    x_s[f, near] = ref[BACK * k + p, at(b), :].astype(F32)
                for f, p in FAR.items():
                    x_s[f, far] = ref[BACK * k + p, at(b), :].astype(F32)

            def back(src, i, kt, ks, with_v):
                te, sa, u, v, pr = (src[f, i] for f in range(5))
                mix = lambda f, x: centre * x + mixing * (src[f, i + 1] + src[f, i - 1] + lanes.both(x))
                q = half * (src[U, i + 1] - src[U, i - 1] + lanes.diff(v))
                gq = gravity * q if gravity != 1.0 else q
                heat = mix(TE, te) + kt * gq
                salt = mix(SA, sa) + ks * gq
                east = u - lanes.rot * v + half * (src[PR, i + 1] - src[PR, i - 1])
                north = v + lanes.rot * u + half * lanes.diff(pr) if with_v else None
                surf = mix(PR, pr) + q
                return heat, salt, east, north, surf

            for c in range(-1, width + 1):
                inside = 0 <= c < width
                if inside:
                    kt, ks = dens_ref[k, 1, 0, c, at(b), :], dens_ref[k, 1, 1, c, at(b), :]
                else:
                    kt, ks = dens(beyond(c, AHEAD * k + H0), beyond(c, AHEAD * k + H1))
                mask = mask_at(c)
                new = back(x_s, c + 2, kt, ks, inside)
                for f in range(5):
                    if new[f] is not None:
                        y_s[f, c + 2] = mask * new[f]
            for c in range(width):
                new = back(y_s, c + 2, dens_ref[k, 0, 0, c, at(b), :], dens_ref[k, 0, 1, c, at(b), :], True)
                for f in range(fields):
                    if k == 0:
                        mult = rows_of(mult_ref, (f,), b, c, width)
                        resid = (
                            rows_of(misfit_ref, (f,), b, c, width)
                            - damp_ref[f, at(b), :] * mult
                            - (rows_of(inc_ref, (0, f), b, c, width) - precede * column_of(prev_in, prev_out, f, b, c, width).astype(F32))
                        )
                        misfit_total = misfit_total + resid * resid
                        value = mult + relaxation * resid
                    else:
                        value = column_of(mnext_in, mnext_out, f, b, c, width)
                    spot = pl.ds(b * (LB * width) + c, LB, stride=width)
                    mult_out[k, f, pl.ds(c, LB, stride=width), :] = value
                    grad = value - new[f]
                    if f < 2:
                        grad = grad + rows_of(spread_ref, (k, f), b, c, width)
                    grad_total = grad_total + grad * grad
                    grad_ref[k, f, spot, :] = grad
        acc_s[0] += misfit_total
        acc_s[1] += grad_total

    body()

    @pl.when(b == pl.num_programs(0) - 1)
    def _():
        misfit_sum = jnp.sum(acc_s[0] + sum_ref[...])
        grad_sum = jnp.sum(acc_s[1])
        lane = lax.broadcasted_iota(jnp.int32, (1, 128), 1)
        scalars = jnp.where(lane == 0, misfit_sum, jnp.where(lane == 1, grad_sum, 0.0))
        pieces = jnp.sum(seen_ref[...], axis=0)
        peers = fin_ref.shape[0]
        for i in range(peers):
            fin_ref[i, 0:1, :] = scalars
            fin_ref[i, 1:, :] = pieces


def step_kernel(recv_ref, inc_ref, grad_ref, mult_ref, innov_ref, err_ref, out_ref, next_ref):
    parts = recv_ref[:, 0, :]
    sums = jnp.sum(parts, axis=0, keepdims=True)
    lane = lax.broadcasted_iota(jnp.int32, sums.shape, 1)
    misfit_square = jnp.sum(jnp.where(lane == 0, sums, 0.0), axis=1, keepdims=True)
    gradient_square = jnp.sum(jnp.where(lane == 1, sums, 0.0), axis=1, keepdims=True)
    stride = misfit_square / (gradient_square + epsilon)
    size = out_ref.shape[2]
    b = pl.program_id(0)
    spot = pl.ds(pl.multiple_of(b * size, size), size)
    for k in range(inc_ref.shape[0]):
        for f in range(inc_ref.shape[1]):
            out_ref[k, f] = inc_ref[k, f, spot, :] - stride * grad_ref[k, f, spot, :]

    @pl.when(b == 0)
    def _():
        subs, nobs = mult_ref.shape
        share = recv_ref.shape[1] - 1
        first = lax.axis_index("tm") * lax.axis_size("space")
        for k in range(subs):
            for i in range(nobs // 128):
                g = k * (nobs // 128) + i
                span = slice(i * 128, (i + 1) * 128)
                seen = recv_ref[first + g // share, 1 + g % share : 2 + g % share, :]
                mult = mult_ref[k : k + 1, span]
                resid = innov_ref[k : k + 1, span] - err_ref[k : k + 1, span] * mult - seen
                next_ref[k : k + 1, span] = mult + relaxation * resid


def shifted(shard, axis, by):
    peers = lax.axis_size(axis)
    return lax.ppermute(shard, axis, [(i, (i + by) % peers) for i in range(peers)])


def swapped(shard, axis, pair):
    peers = lax.axis_size(axis)
    ahead = 0 if pair else 1
    return lax.ppermute(shard, axis, [(i, (i + (1 if i % 2 == ahead else -1)) % peers) for i in range(peers)])


def within(
    increment, multiplier, sensor_multiplier, misfit, innovation,
    model_error, sensor_error, trajectory, land_sea, sensor_cells,
):
    subs, fields, levels, width, latitude = increment.shape
    nobs = sensor_cells.shape[1]
    teams, tiles = lax.axis_size("tm"), lax.axis_size("space")
    peers = teams * tiles
    share = subs * nobs // (128 * tiles)
    assert tiles % 2 == 0 and fields == 5 and trajectory.shape[1] == 2 and subs == 2 and levels % LB == 0 and width >= 6
    assert latitude == 128 and (width * tiles) & (width * tiles - 1) == 0 and nobs % 512 == 0
    assert share * 128 * tiles == subs * nobs and (2 * levels * width) % 32 == 0
    rows = levels * width
    fast = lambda x: pltpu.with_memory_space_constraint(x, pltpu.VMEM)
    slow = lambda x: pltpu.with_memory_space_constraint(x, pltpu.HBM)
    native_shape = (subs, fields, rows, latitude)
    inc = slow(increment.reshape(native_shape))
    traj = slow(trajectory.reshape(subs, 2, 2, rows, latitude))
    mult = slow(multiplier.reshape(native_shape))
    mis = slow(misfit.reshape(native_shape))
    cells, sen_m, sen_i, sen_e = (fast(x) for x in (sensor_cells, sensor_multiplier, innovation, sensor_error))
    vmem = pl.BlockSpec(memory_space=pltpu.VMEM)
    hbm = pl.BlockSpec(memory_space=pltpu.HBM)
    scr = lambda *s: pltpu.VMEM(s, F32)
    limit = pltpu.CompilerParams(vmem_limit_bytes=VMEM_LIMIT)

    def call(kernel, outs, scratch, *args, specs=None):
        return pl.pallas_call(
            kernel,
            in_specs=specs or [vmem] * len(args),
            out_specs=[vmem] * len(outs),
            out_shape=[pltpu.VMEM(s, d) for s, d in outs],
            scratch_shapes=scratch,
            compiler_params=limit,
        )(*args)

    ahead = (subs * AHEAD + 1, levels, latitude)
    one = native_shape[1:]
    inc, traj, mult0, mis0, land, pair, link, edge, inner, damp = call(
        load_kernel,
        [
            (native_shape, F32), (traj.shape, BF16), (one, F32), (one, F32), (land_sea.shape, jnp.int32),
            (ahead, BF16), (ahead, BF16),
            ((fields, 4, levels, latitude), BF16),
            ((fields, width - 4, levels, latitude), BF16),
            ((fields, levels, latitude), F32),
        ],
        [
            pltpu.SMEM(model_error.shape, F32), scr(4, LB * width, latitude),
            pltpu.SemaphoreType.DMA((4, levels // LB)), pltpu.SemaphoreType.DMA((2,)),
        ],
        slow(model_error), inc, traj, mult, mis, slow(land_sea),
        specs=[hbm] * 6,
    )
    link_in = fast(swapped(link, "space", False))
    pair_in = fast(swapped(pair, "space", True))
    edge_in = fast(shifted(edge, "tm", -1))
    inner_in = fast(shifted(inner, "tm", -1))

    seen, spread, sensor_sum, density, mult1, mis1 = call(
        lambda *refs: sensor_kernel(*refs, columns=width * tiles),
        [
            ((tiles, share, 128), F32), ((subs, 2 * rows, latitude), F32), ((1, 512), F32),
            ((subs, 2, 2, width, levels, latitude), F32), (one, F32), (one, F32),
        ],
        [
            pltpu.VMEM((2 * rows, nobs), BF16), pltpu.VMEM((2 * latitude, nobs), BF16), scr(2, LB * width, latitude),
            pltpu.SemaphoreType.DMA((2,)),
        ],
        inc, cells, sen_m, sen_i, sen_e, traj, mult, mis,
        specs=[vmem] * 6 + [hbm] * 2,
    )
    spread = spread.reshape(subs, 2, rows, latitude)
    seen_in = fast(lax.all_to_all(seen, "space", 0, 0))

    outside, within_it = (fields, 4, levels, latitude), (fields, width - 4, levels, latitude)
    behind = (subs * BACK, levels, latitude)
    strip = lambda n: scr(n, width + 4, LB, latitude)
    mid, fwd_in, send_in, mnext_in, sums = call(
        interior_kernel,
        [((subs, 6, 4, levels, latitude), F32), (within_it, F32), (within_it, BF16), (within_it, F32), ((LB, latitude), F32)],
        [strip(5), strip(6), scr(width + 4, LB, latitude)],
        inc, density, land, mult1, mis1, damp, sensor_sum,
    )
    prev_in = fast(shifted(send_in, "tm", 1))
    fwd_out, send_out, mnext_out, back_pair, back_link, sums = call(
        edge_kernel,
        [(outside, F32), (outside, BF16), (outside, F32), (behind, BF16), (behind, BF16), ((LB, latitude), F32)],
        [strip(5), strip(6), scr(width + 4, LB, latitude), scr(2, subs * BACK, LB, latitude)],
        inc, density, land, pair_in, link_in, mult1, mis1, damp, edge_in, mid, sums,
    )
    back_link_in = fast(swapped(back_link, "space", False))
    back_pair_in = fast(swapped(back_pair, "space", True))
    prev_out = fast(shifted(send_out, "tm", 1))

    block = pl.BlockSpec((subs, fields, LB * width, latitude), lambda i: (0, 0, i, 0))
    mult_next, gradient, final = pl.pallas_call(
        adjoint_kernel,
        name="adjoint",
        grid=(levels // LB,),
        in_specs=[vmem] * 21,
        out_specs=[block, vmem, vmem],
        out_shape=[
            jax.ShapeDtypeStruct(native_shape, F32),
            pltpu.VMEM(native_shape, F32),
            pltpu.VMEM((peers, 1 + share, 128), F32),
        ],
        scratch_shapes=[scr(5, width + 4, LB, latitude), scr(5, width + 4, LB, latitude), scr(2, LB, latitude)],
        compiler_params=limit,
    )(
        inc, density, land, pair_in, link_in, back_pair_in, back_link_in, mult0, mis0, damp,
        fwd_in, fwd_out, mnext_in, mnext_out, edge_in, inner_in, prev_in, prev_out, spread, sums, seen_in,
    )
    final = fast(lax.all_to_all(final, ("tm", "space"), 0, 0))

    steps = 4 if rows % 32 == 0 else 1
    size = rows // steps
    increment_next, sensor_next = pl.pallas_call(
        lambda *refs: step_kernel(*refs),
        name="step",
        grid=(steps,),
        in_specs=[vmem] * 6,
        out_specs=[
            pl.BlockSpec((subs, fields, size, latitude), lambda i: (0, 0, i, 0)),
            pl.BlockSpec((subs, nobs), lambda i: (0, 0)),
        ],
        out_shape=[
            jax.ShapeDtypeStruct(native_shape, F32),
            jax.ShapeDtypeStruct((subs, nobs), F32),
        ],
        compiler_params=limit,
    )(final, inc, gradient, sen_m, sen_i, sen_e)
    return (increment_next.reshape(increment.shape), mult_next.reshape(multiplier.shape), sensor_next)


def solution(mesh):
    state = P("tm", None, None, "space", None)
    placed = (
        state,
        state,
        P("tm", None),
        state,
        P("tm", None),
        P(),
        P("tm", None),
        P("tm", None, None, None, "space", None),
        P("space", None),
        P("tm", None),
    )
    return jax.shard_map(
        within,
        mesh=mesh,
        in_specs=placed,
        out_specs=(state, state, P("tm", None)),
        check_vma=False,
    )
```
